32 devices in a mesh: dom: 32 (over z, y, x, core).
Axes of the slice: x: 2, y: 2, z: 4, core: 2. Of those that a mesh axis runs over, the one named last changes fastest.
Arguments:
- features: bfloat16 [65536, 256], P('dom'), may hold values from -6 to 6
- self_weight: bfloat16 [256, 256], replicated, may hold values from -0.375 to 0.375
- neighbour_weight: bfloat16 [256, 256], replicated, may hold values from -0.375 to 0.375
- send_lists: int32 [32, 32, 8], P('dom'), may hold values from 0 to 2047
- hub_nodes: int32 [32, 8], P('dom'), may hold values from 0 to 2047
- neighbours: int32 [65536, 16], P('dom'), may hold values from 0 to 2559
- counts: int32 [65536], P('dom'), may hold values from 1 to 16
- cotangent: bfloat16 [65536, 256], P('dom'), may hold values from -6 to 6
Outputs:
- activations: bfloat16 [65536, 256], P('dom')
- grad_features: float32 [65536, 256], P('dom')
- grad_weights: float32 [512, 256], P('dom')
The draws below stay inside these ranges and needn't reach their ends.
All inputs are finite; a program needn't handle non-finite values.
Results may differ from the reference program's by a relative error of at most 0.0032.
Values may be sent and summed in bfloat16 or wider, within the bound.
A program may use at most 64 MiB of HBM per device.

```python
import jax
import jax.numpy as jnp
from jax import lax

F = 256
H = 256
FAN = 16
NODE_DEV = 2048
BND = 8
HUB_DEV = 8
NODES = 65536
TABLE = 2560
N_DOM = 32


def place_ends(drawn, stream_key, least, largest):
    index_at = [jax.random.randint(jax.random.fold_in(stream_key, axis), (), 0, length) for axis, length in enumerate(drawn.shape)]
    longest = drawn.shape.index(max(drawn.shape))
    beside = index_at[:longest] + [(index_at[longest] + 1) % drawn.shape[longest]] + index_at[longest + 1:]
    return drawn.at[tuple(index_at)].set(least).at[tuple(beside)].set(largest)


def raised(result, rng, source, target, parts, factor):
    owner, partner = [(jnp.arange(result.shape[dim]) // (result.shape[dim] // parts)).reshape([-1 if axis == dim else 1 for axis in range(result.ndim)]) for dim in (source, target)]
    chosen = jax.random.permutation(rng, parts)[partner]
    strong = (owner == chosen) | (owner == (partner + parts // 2) % parts)
    return jnp.where(strong, factor * result, result)


def block_levels(own_key, shape, shards, least, high):
    level, own = 1.0, jax.random.fold_in(own_key, 6)
    for position, blocks in shards:
        draws = jnp.exp(jax.random.uniform(jax.random.fold_in(own, position), (blocks,), jnp.float32, least / len(shards), high / len(shards)))
        level = level * jnp.repeat(draws, shape[position] // blocks).reshape([-1 if axis == position else 1 for axis in range(len(shape))])
    return level


def bell_draw(stream_key, shape, spread, limit, pieces=(), kind=jnp.bfloat16):
    array = jax.random.normal(stream_key, shape, jnp.float32) * spread
    if len(pieces) > 0:
        array = block_levels(stream_key, shape, pieces, -0.22, 0.18) * array
    return jnp.clip(array, min=-limit, max=limit).astype(kind)


def noise_with(key, extent, width, limit, shards, heavy, held_as=jnp.bfloat16):
    result = width * jax.random.normal(key, extent, jnp.float32)
    if shards:
        result = result * block_levels(key, extent, shards, -0.22, 0.18)
    return jnp.clip(raised(result, jax.random.fold_in(key, 3), *heavy), -limit, limit).astype(held_as)


def setup_inputs(seed: int = 0) -> dict:
    splits = jax.random.split(jax.random.key(seed), 9)
    features = noise_with(splits[0], (NODES, F), 1.0, 6.0, ((0, 32),), (0, 1, 32, 2.75))
    self_weight = bell_draw(splits[1], (F, H), F ** -0.5, 0.375)
    neighbour_weight = bell_draw(splits[2], (F, H), F ** -0.5, 0.375)
    send_lists = place_ends(jax.random.randint(splits[3], (N_DOM, N_DOM, BND), 0, NODE_DEV), jax.random.fold_in(splits[3], 1), 0, NODE_DEV - 1).astype(jnp.int32)
    hub_nodes = place_ends(jax.random.randint(splits[4], (N_DOM, HUB_DEV), 0, NODE_DEV), jax.random.fold_in(splits[4], 1), 0, NODE_DEV - 1).astype(jnp.int32)
    neighbours = place_ends(jax.random.randint(splits[5], (NODES, FAN), 0, TABLE), jax.random.fold_in(splits[5], 1), 0, TABLE - 1).astype(jnp.int32)
    counts = place_ends(jax.random.randint(splits[6], (NODES,), 1, FAN + 1), jax.random.fold_in(splits[6], 1), 1, FAN).astype(jnp.int32)
    cotangent = bell_draw(splits[7], (NODES, H), 1.0, 6.0, ((0, 32),))
    return dict(features=features, self_weight=self_weight, neighbour_weight=neighbour_weight, send_lists=send_lists, hub_nodes=hub_nodes, neighbours=neighbours, counts=counts, cotangent=cotangent)


def resolve(send_lists, hub_nodes, neighbours):
    partition = (jnp.arange(NODES, dtype=jnp.int32) // NODE_DEV)[:, None]
    table_slot = neighbours
    bound_slot = table_slot - NODE_DEV
    bound_peer = jnp.clip(bound_slot // BND, 0, N_DOM - 1)
    bound_pos = bound_slot % BND
    flat_lists = send_lists.reshape(-1)
    bound_index = (bound_peer * (N_DOM * BND) + partition * BND + bound_pos).astype(jnp.int32)
    bound_source = bound_peer * NODE_DEV + jnp.take(flat_lists, bound_index)
    hub_slot = table_slot - NODE_DEV - N_DOM * BND
    hub_owner = jnp.clip(hub_slot // HUB_DEV, 0, N_DOM - 1)
    hub_index = (hub_owner * HUB_DEV + hub_slot % HUB_DEV).astype(jnp.int32)
    hub_source = hub_owner * NODE_DEV + jnp.take(hub_nodes.reshape(-1), hub_index)
    local_source = partition * NODE_DEV + table_slot
    source = jnp.where(table_slot < NODE_DEV, local_source,
                       jnp.where(table_slot < NODE_DEV + N_DOM * BND, bound_source, hub_source))
    return source.astype(jnp.int32)


def reference(features, self_weight, neighbour_weight, send_lists, hub_nodes, neighbours, counts, cotangent):
    source = resolve(send_lists, hub_nodes, neighbours)
    usable = jnp.arange(FAN, dtype=jnp.int32)[None, :] < counts[:, None]
    degree = counts.astype(jnp.float32)[:, None]
    blocked_source = source.reshape(N_DOM, NODE_DEV, FAN)
    blocked_usable = usable.reshape(N_DOM, NODE_DEV, FAN)
    blocked_degree = degree.reshape(N_DOM, NODE_DEV, 1)

    def mean_block(block_args):
        block_source, block_usable, block_degree = block_args
        gathered = jnp.take(features, block_source, axis=0).astype(jnp.float32)
        summed = jnp.sum(jnp.where(block_usable[:, :, None], gathered, 0.0), axis=1)
        return (summed / block_degree).astype(jnp.bfloat16)

    mean = lax.map(mean_block, (blocked_source, blocked_usable, blocked_degree)).reshape(NODES, F)
    pre = jnp.dot(features, self_weight, preferred_element_type=jnp.float32) + jnp.dot(mean, neighbour_weight, preferred_element_type=jnp.float32)
    sigmoid_pre = jax.nn.sigmoid(pre)
    activations = (pre * sigmoid_pre).astype(jnp.bfloat16)
    grad_pre = (cotangent.astype(jnp.float32) * sigmoid_pre * (1.0 + pre * (1.0 - sigmoid_pre))).astype(jnp.bfloat16)
    grad_mean = jnp.dot(grad_pre, neighbour_weight.T, preferred_element_type=jnp.float32)
    grad_self = jnp.dot(grad_pre, self_weight.T, preferred_element_type=jnp.float32)
    edge_weight = (grad_mean / degree).reshape(N_DOM, NODE_DEV, F)

    def add_block(grad_total, block_args):
        block_source, block_usable, block_weight = block_args
        contrib = jnp.where(block_usable[:, :, None], block_weight[:, None, :], 0.0).reshape(-1, F)
        return grad_total.at[block_source.reshape(-1)].add(contrib), None

    grad_features, unused = lax.scan(add_block, grad_self, (blocked_source, blocked_usable, edge_weight))
    dims = (((0,), (0,)), ((), ()))
    upper = lax.dot_general(features, grad_pre, dims, preferred_element_type=jnp.float32)
    lower = lax.dot_general(mean, grad_pre, dims, preferred_element_type=jnp.float32)
    grad_weights = jnp.concatenate([upper, lower], axis=0)
    return activations, grad_features, grad_weights
```

```python
import functools

import jax
import jax.numpy as jnp
from jax import lax
from jax.experimental import pallas as pl
from jax.experimental.pallas import tpu as pltpu
from jax.sharding import PartitionSpec as P

LO = 256
LANES = 128
BLOCK = 256
GROUP = 16
BF16 = jnp.bfloat16
F32 = jnp.float32
F8 = jnp.float8_e4m3fn
MESH = pl.DeviceIdType.MESH


def dot(a, b, ca, cb):
    return lax.dot_general(a, b, (((ca,), (cb,)), ((), ())), preferred_element_type=F32)


def split(peers):
    half = peers // 2
    inner = 1
    while inner * inner < half:
        inner *= 2
    return half // inner, inner


def halves(rows):
    count, width = rows.shape[0] // 8, rows.shape[1] // LANES
    return jnp.concatenate(
        [rows[:, i * LANES : (i + 1) * LANES].reshape(count, 8, LANES) for i in range(width)], axis=1
    )


def joined(tiles):
    count, width = tiles.shape[0], tiles.shape[1] // 8
    return jnp.concatenate(
        [tiles[:, i * 8 : (i + 1) * 8].reshape(count * 8, LANES) for i in range(width)], axis=1
    )


def whole_kernel(
    peers,
    neighbours_in, counts_in, lists_in, hubs_in, features_in, cotangent_in, self_in, neighbour_in,
    activations_out, grads_out, weight_out_ref,
    index_ref, counts_ref, lists_ref, hubs_ref, features_ref, cotangent_ref, self_ref, neighbour_ref,
    picks, rows_send, rows_in, high_rows, low_rows, count, summed, mean_all, grad_t, edge_rows, edge_t,
    activations_ref, out_ref, part_send, part_in, pair_send, pair_in, inner_send, inner_in,
    outer_send, outer_in,
    in_sem, row_sem, part_sem, pair_sem, inner_sem, outer_sem, out_sem,
):
    me = lax.axis_index("dom")
    outer, inner = split(peers)
    core = me % 2
    my_inner = (me // 2) % inner
    my_outer = me // (2 * inner)
    nodes, width = features_ref.shape
    fan = index_ref.shape[0]
    per_peer = lists_ref.shape[0]
    hubs = hubs_ref.shape[1]
    bound = peers * per_peer
    groups = nodes // GROUP
    blocks = count.shape[1] // LO
    share = weight_out_ref.shape[0]

    ins = (
        (lists_in, lists_ref), (hubs_in, hubs_ref), (features_in, features_ref),
        (neighbours_in, index_ref), (counts_in, counts_ref), (self_in, self_ref),
        (neighbour_in, neighbour_ref), (cotangent_in, cotangent_ref),
    )
    loads = [pltpu.make_async_copy(a, b, in_sem.at[i]) for i, (a, b) in enumerate(ins)]
    for load in loads:
        load.start()

    barrier = pltpu.get_barrier_semaphore()

    @pl.loop(1, peers)
    def _(p):
        pl.semaphore_signal(
            barrier, inc=1, device_id=(lax.rem(me + p, peers),), device_id_type=MESH
        )

    one = jnp.ones((), BF16)
    zero = jnp.zeros((), BF16)

    loads[0].wait()
    loads[1].wait()
    owner = jnp.where(
        lax.broadcasted_iota(jnp.int32, (bound, peers), 0) // per_peer
        == lax.broadcasted_iota(jnp.int32, (bound, peers), 1), 1.0, 0.0,
    ).astype(BF16)
    own_slot = (
        lax.broadcasted_iota(jnp.int32, (bound, per_peer), 0) % per_peer
        == lax.broadcasted_iota(jnp.int32, (bound, per_peer), 1)
    )
    own_hub = (
        lax.broadcasted_iota(jnp.int32, (2 * hubs, hubs), 0) % hubs
        == lax.broadcasted_iota(jnp.int32, (2 * hubs, hubs), 1)
    )
    spread_hubs = jnp.broadcast_to(hubs_ref[...], (2 * hubs, hubs))

    def digit(take):
        sent = take(lists_ref[...]).astype(F32).astype(BF16)
        rows = jnp.sum(jnp.where(own_slot, dot(owner, sent, 1, 1), 0.0), axis=1, keepdims=True)
        hub = jnp.sum(
            jnp.where(own_hub, take(spread_hubs).astype(F32), 0.0), axis=1, keepdims=True
        )
        column = jnp.concatenate([rows, hub], axis=0)
        return jnp.broadcast_to(column, (bound + 2 * hubs, LO)).astype(BF16)

    list_high, list_low = digit(lambda v: v >> 8), digit(lambda v: v & (LO - 1))
    lane = lax.broadcasted_iota(jnp.int32, (bound + 2 * hubs, LO), 1).astype(F32).astype(BF16)
    for h in range(nodes // LO):
        low = jnp.where(list_high == jnp.full((), h, BF16), list_low, -one)
        picks[:, h * LO : (h + 1) * LO] = jnp.where(low == lane, one, zero)
    loads[2].wait()
    packed = dot(picks[...], features_ref[...], 1, 0)
    hub_tile = halves(packed[bound : bound + hubs])
    rows_send[...] = jnp.concatenate(
        [halves(packed[:bound]), jnp.broadcast_to(hub_tile, (peers, 16, LANES))], axis=1
    ).astype(BF16)
    rows_in[me] = rows_send[me]
    pl.semaphore_wait(barrier, peers - 1)

    @pl.loop(1, peers)
    def _(p):
        peer = lax.rem(me + p, peers)
        pltpu.make_async_remote_copy(
            src_ref=rows_send.at[peer], dst_ref=rows_in.at[me],
            send_sem=row_sem.at[0], recv_sem=row_sem.at[1],
            device_id=(peer,), device_id_type=MESH,
        ).start()

    loads[3].wait()
    loads[4].wait()
    usable = lax.broadcasted_iota(jnp.int32, (fan, nodes), 0) < counts_ref[...]
    index = jnp.where(usable, index_ref[...], -1)
    stacked = jnp.concatenate(
        [index[:, j * groups : (j + 1) * groups] for j in range(GROUP)], axis=0
    )
    high_rows[...] = (stacked >> 8).astype(F32).T
    low_rows[...] = (stacked & (LO - 1)).astype(F32).T
    pairs = GROUP * fan
    mine = (
        lax.broadcasted_iota(jnp.int32, (GROUP, pairs), 0)
        == lax.broadcasted_iota(jnp.int32, (GROUP, pairs), 1) // fan
    )
    low_ids = lax.broadcasted_iota(jnp.int32, (LO, pairs), 0).astype(F32).astype(BF16)

    @pl.loop(0, groups // 16)
    def _(step):
        at16 = pl.ds(pl.multiple_of(step * 16, 16), 16)
        highs, lows = high_rows[at16, :], low_rows[at16, :]
        for group in range(16):
            high = jnp.broadcast_to(highs[group : group + 1, :], (GROUP, pairs)).astype(BF16)
            high = jnp.where(mine, high, -one)
            low = jnp.broadcast_to(lows[group : group + 1, :], (16, pairs)).astype(BF16)
            low = jnp.concatenate([low] * (LO // 16), axis=0)
            low_hot = jnp.where(low_ids == low, one, zero).astype(F8)
            high_hot = jnp.concatenate(
                [jnp.where(high == jnp.full((), h, BF16), one, zero) for h in range(blocks)],
                axis=0,
            ).astype(F8)
            counted = dot(high_hot, low_hot, 1, 1).astype(BF16)
            at = pl.ds(pl.multiple_of(step * 256 + 16 * group, 16), 16)
            for h in range(blocks):
                count[at, h * LO : (h + 1) * LO] = counted[16 * h : 16 * h + 16]

    total = dot(count[:, :nodes], features_ref[...], 1, 0)
    for i in range(width // LANES):
        summed[i] = total[:, i * LANES : (i + 1) * LANES]

    others = pl.ds(0, peers - 1)
    pltpu.make_async_copy(rows_in.at[others], rows_in.at[others], row_sem.at[1]).wait()
    arrived = rows_in[...].astype(F32)
    table = jnp.concatenate([joined(arrived[:, :16]), joined(arrived[:, 16:])], axis=0)
    total = dot(count[:, nodes:], table.astype(BF16), 1, 0)
    for i in range(width // LANES):
        summed[i] = summed[i] + total[:, i * LANES : (i + 1) * LANES]

    for load in loads[5:]:
        load.wait()
    inverse = 1.0 / counts_ref[...].astype(F32)
    for j in range(GROUP):
        at = slice(j * groups, (j + 1) * groups)
        column = jnp.broadcast_to(inverse[:, at], (LANES, groups)).T
        strided = pl.ds(j, groups, stride=GROUP)
        mean = jnp.concatenate(
            [summed[i, strided, :] * column for i in range(width // LANES)], axis=1
        ).astype(BF16)
        mean_all[at, :] = mean
        pre = dot(features_ref[at, :], self_ref[...], 1, 0) + dot(mean, neighbour_ref[...], 1, 0)
        sig = jax.nn.sigmoid(pre)
        activations_ref[at, :] = (pre * sig).astype(BF16)
        grad_pre = (
            cotangent_ref[at, :].astype(F32) * sig * (1.0 + pre * (1.0 - sig))
        ).astype(BF16)
        grad_t[:, at] = grad_pre.T
        edge = dot(grad_pre, neighbour_ref[...], 1, 1)
        for i in range(width // LANES):
            edge_rows[i, strided, :] = edge[:, i * LANES : (i + 1) * LANES] * column
    act_copy = pltpu.make_async_copy(activations_ref, activations_out, out_sem.at[0])
    act_copy.start()
    for i in range(width // LANES):
        edge_t[i * LANES : (i + 1) * LANES, :] = edge_rows[i].astype(BF16).T

    hub_part = halves(dot(edge_t[...], count[:, nodes + bound :], 1, 0).T)
    upper = dot(grad_t[...], features_ref[...], 1, 0).T
    lower = dot(grad_t[...], mean_all[...], 1, 0).T
    for o in range(peers):
        at = (o % 2, (o // 2) % inner, o // (2 * inner))
        source = upper if o * share < width else lower
        start = o * share % width
        for i in range(width // LANES):
            pair_send[at + (slice(i * share, (i + 1) * share),)] = source[
                start : start + share, i * LANES : (i + 1) * LANES
            ]
        pair_send[at + (slice(2 * share, 2 * share + 16),)] = hub_part[o]
    pair_copy = pltpu.make_async_remote_copy(
        src_ref=pair_send.at[1 - core], dst_ref=pair_in,
        send_sem=pair_sem.at[0], recv_sem=pair_sem.at[1],
        device_id=(me + 1 - 2 * core,), device_id_type=MESH,
    )
    pair_copy.start()

    bound_part = dot(edge_t[...], count[:, nodes : nodes + bound], 1, 0).T
    part_send[...] = halves(bound_part).astype(BF16)
    part_in[me] = part_send[me]

    @pl.loop(1, peers)
    def _(p):
        peer = lax.rem(me + p, peers)
        pltpu.make_async_remote_copy(
            src_ref=part_send.at[peer], dst_ref=part_in.at[me],
            send_sem=part_sem.at[0], recv_sem=part_sem.at[1],
            device_id=(peer,), device_id_type=MESH,
        ).start()

    pair_copy.wait_recv()
    inner_send[...] = (pair_send[core] + pair_in[...]).astype(BF16)

    @pl.loop(1, inner)
    def _(p):
        to = lax.rem(my_inner + p, inner)
        pltpu.make_async_remote_copy(
            src_ref=inner_send.at[to], dst_ref=inner_in.at[my_inner],
            send_sem=inner_sem.at[0], recv_sem=inner_sem.at[1],
            device_id=((my_outer * inner + to) * 2 + core,), device_id_type=MESH,
        ).start()

    def local(first, last):
        at = slice(first * LO, last * LO)
        part = dot(edge_t[...], count[:, at], 1, 0) + dot(self_ref[...], grad_t[:, at], 1, 0)
        out_ref[at, :] = part.T

    local_blocks = nodes // LO
    local(0, local_blocks // 2)

    inner_others = pl.ds(0, inner - 1)
    own_inner = pair_send[core, my_inner] + pair_in[my_inner]
    inner_in[my_inner] = jnp.zeros(inner_in.shape[1:], BF16)
    pltpu.make_async_copy(
        inner_in.at[inner_others], inner_in.at[inner_others], inner_sem.at[1]
    ).wait()
    inner_sum = own_inner + jnp.sum(inner_in[...].astype(F32), axis=0)
    pair_in[0] = inner_sum
    outer_send[...] = inner_sum.astype(BF16)

    @pl.loop(1, outer)
    def _(p):
        to = lax.rem(my_outer + p, outer)
        pltpu.make_async_remote_copy(
            src_ref=outer_send.at[to], dst_ref=outer_in.at[my_outer],
            send_sem=outer_sem.at[0], recv_sem=outer_sem.at[1],
            device_id=((to * inner + my_inner) * 2 + core,), device_id_type=MESH,
        ).start()

    local(local_blocks // 2, local_blocks)

    outer_others = pl.ds(0, outer - 1)
    outer_in[my_outer] = jnp.zeros(outer_in.shape[1:], BF16)
    pltpu.make_async_copy(part_in.at[others], part_in.at[others], part_sem.at[1]).wait()
    pltpu.make_async_copy(
        outer_in.at[outer_others], outer_in.at[outer_others], outer_sem.at[1]
    ).wait()
    total = pair_in[0, my_outer] + jnp.sum(outer_in[...].astype(F32), axis=0)
    for i in range(width // LANES):
        weight_out_ref[:, i * LANES : (i + 1) * LANES] = total[i * share : (i + 1) * share]
    hub_sum = joined(total[None, 2 * share :])
    hub_high = hub_sum.astype(BF16).astype(F32)
    returned = jnp.concatenate(
        [joined(part_in[...].astype(F32)), hub_high, hub_sum - hub_high], axis=0
    ).astype(BF16).T
    for h in range(local_blocks):
        at = slice(h * LO, (h + 1) * LO)
        out_ref[at, :] = out_ref[at, :] + dot(returned, picks[:, at], 1, 0).T
        pltpu.make_async_copy(out_ref.at[at], grads_out.at[at], out_sem.at[1]).start()

    pltpu.make_async_copy(rows_send.at[others], rows_send.at[others], row_sem.at[0]).wait()
    pltpu.make_async_copy(part_send.at[others], part_send.at[others], part_sem.at[0]).wait()
    pair_copy.wait_send()
    pltpu.make_async_copy(
        inner_send.at[inner_others], inner_send.at[inner_others], inner_sem.at[0]
    ).wait()
    pltpu.make_async_copy(
        outer_send.at[outer_others], outer_send.at[outer_others], outer_sem.at[0]
    ).wait()
    act_copy.wait()
    pltpu.make_async_copy(out_ref, grads_out, out_sem.at[1]).wait()


def body(
    features, self_weight, neighbour_weight, send_lists, hub_nodes, neighbours, counts, cotangent
):
    nodes, width = features.shape
    fan = neighbours.shape[1]
    peers = lax.axis_size("dom")
    per_peer = send_lists.shape[2]
    hubs = hub_nodes.shape[1]
    bound = peers * per_peer
    columns = nodes + bound + peers * hubs
    share = 2 * width // peers
    outer, inner = split(peers)
    terms = 2 * share + 16
    dma = pltpu.SemaphoreType.DMA
    return pl.pallas_call(
        functools.partial(whole_kernel, peers),
        in_specs=[pl.BlockSpec(memory_space=pl.ANY)] * 8,
        out_specs=[pl.BlockSpec(memory_space=pl.ANY)] * 2 + [pl.BlockSpec(memory_space=pltpu.VMEM)],
        out_shape=[
            jax.ShapeDtypeStruct((nodes, width), BF16),
            jax.ShapeDtypeStruct((nodes, width), F32),
            jax.ShapeDtypeStruct((share, width), F32),
        ],
        scratch_shapes=[
            pltpu.VMEM((fan, nodes), jnp.int32),
            pltpu.VMEM((1, nodes), jnp.int32),
            pltpu.VMEM((per_peer, peers), jnp.int32),
            pltpu.VMEM((1, hubs), jnp.int32),
            pltpu.VMEM((nodes, width), BF16),
            pltpu.VMEM((nodes, width), BF16),
            pltpu.VMEM((width, width), BF16),
            pltpu.VMEM((width, width), BF16),
            pltpu.VMEM((bound + 2 * hubs, nodes), BF16),
            pltpu.VMEM((peers, 32, LANES), BF16),
            pltpu.VMEM((peers, 32, LANES), BF16),
            pltpu.VMEM((nodes // GROUP, GROUP * fan), F32),
            pltpu.VMEM((nodes // GROUP, GROUP * fan), F32),
            pltpu.VMEM((nodes, columns), BF16),
            pltpu.VMEM((width // LANES, nodes, LANES), F32),
            pltpu.VMEM((nodes, width), BF16),
            pltpu.VMEM((width, nodes), BF16),
            pltpu.VMEM((width // LANES, nodes, LANES), F32),
            pltpu.VMEM((width, nodes), BF16),
            pltpu.VMEM((nodes, width), BF16),
            pltpu.VMEM((nodes, width), F32),
            pltpu.VMEM((peers, 16, LANES), BF16),
            pltpu.VMEM((peers, 16, LANES), BF16),
            pltpu.VMEM((2, inner, outer, terms, LANES), F32),
            pltpu.VMEM((inner, outer, terms, LANES), F32),
            pltpu.VMEM((inner, outer, terms, LANES), BF16),
            pltpu.VMEM((inner, outer, terms, LANES), BF16),
            pltpu.VMEM((outer, terms, LANES), BF16),
            pltpu.VMEM((outer, terms, LANES), BF16),
            dma((8,)), dma((2,)), dma((2,)), dma((2,)), dma((2,)), dma((2,)), dma((2,)),
        ],
        compiler_params=pltpu.CompilerParams(
            collective_id=0, has_side_effects=True, vmem_limit_bytes=60 * 1024 * 1024
        ),
        name="whole",
    )(
        neighbours.T, counts[None, :], send_lists[0].T, hub_nodes, features, cotangent, self_weight,
        neighbour_weight,
    )


def solution(mesh):
    in_specs = (
        P("dom", None),
        P(),
        P(),
        P("dom", None, None),
        P("dom", None),
        P("dom", None),
        P("dom"),
        P("dom", None),
    )
    out_specs = (P("dom", None), P("dom", None), P("dom", None))
    return jax.shard_map(body, mesh=mesh, in_specs=in_specs, out_specs=out_specs, check_vma=False)
```

```python
import functools

import jax
import jax.numpy as jnp
from jax import lax
from jax.experimental import pallas as pl
from jax.experimental.pallas import tpu as pltpu
from jax.sharding import PartitionSpec as P

LO = 256
LANES = 128
VMEM_MAIN = 60
FINISH_STEPS = 4
GROUP = 16
BF16 = jnp.bfloat16
F32 = jnp.float32
F8 = jnp.float8_e4m3fn
MESH = pl.DeviceIdType.MESH


def dot(a, b, ca, cb):
    return lax.dot_general(a, b, (((ca,), (cb,)), ((), ())), preferred_element_type=F32)


def split(peers):
    half = peers // 2
    inner = 1
    while inner * inner < half:
        inner *= 2
    return half // inner, inner


def halves(rows):
    count, width = rows.shape[0] // 8, rows.shape[1] // LANES
    return jnp.concatenate(
        [rows[:, i * LANES : (i + 1) * LANES].reshape(count, 8, LANES) for i in range(width)], axis=1
    )


def joined(tiles):
    count, width = tiles.shape[0], tiles.shape[1] // 8
    return jnp.concatenate(
        [tiles[:, i * 8 : (i + 1) * 8].reshape(count * 8, LANES) for i in range(width)], axis=1
    )


def whole_kernel(
    peers,
    neighbours_in, counts_in, lists_in, hubs_in, features_in, cotangent_in, self_in, neighbour_in,
    activations_out, base_out, picks_out, returned_out, weight_out,
    index_ref, counts_ref, lists_ref, hubs_ref, features_ref, cotangent_ref, self_ref, neighbour_ref,
    picks, rows_send, rows_in, high_rows, low_rows, count, summed, mean_all, grad_t, edge_rows, edge_t,
    activations_ref, base, returned_t, weight_sum, part_send, part_in,
    pair_send, pair_in, inner_send, inner_in, hub_pair_send, hub_pair_in, hub_inner_send, hub_inner_in,
    outer_send, outer_in,
    in_sem, row_sem, part_sem, pair_sem, inner_sem, hub_pair_sem, hub_inner_sem, outer_sem, out_sem,
):
    me = lax.axis_index("dom")
    outer, inner = split(peers)
    core = me % 2
    my_inner = (me // 2) % inner
    my_outer = me // (2 * inner)
    nodes, width = features_ref.shape
    fan = index_ref.shape[0]
    per_peer = lists_ref.shape[0]
    hubs = hubs_ref.shape[1]
    bound = peers * per_peer
    groups = nodes // GROUP
    blocks = count.shape[1] // LO
    share = weight_sum.shape[0]

    ins = (
        (lists_in, lists_ref), (hubs_in, hubs_ref), (features_in, features_ref),
        (neighbours_in, index_ref), (counts_in, counts_ref), (self_in, self_ref),
        (neighbour_in, neighbour_ref), (cotangent_in, cotangent_ref),
    )
    loads = [pltpu.make_async_copy(a, b, in_sem.at[i]) for i, (a, b) in enumerate(ins)]
    for load in loads:
        load.start()

    barrier = pltpu.get_barrier_semaphore()

    @pl.loop(1, peers)
    def _(p):
        pl.semaphore_signal(
            barrier, inc=1, device_id=(lax.rem(me + p, peers),), device_id_type=MESH
        )

    one = jnp.ones((), BF16)
    zero = jnp.zeros((), BF16)

    loads[0].wait()
    loads[1].wait()
    owner = jnp.where(
        lax.broadcasted_iota(jnp.int32, (bound, peers), 0) // per_peer
        == lax.broadcasted_iota(jnp.int32, (bound, peers), 1), 1.0, 0.0,
    ).astype(BF16)
    own_slot = (
        lax.broadcasted_iota(jnp.int32, (bound, per_peer), 0) % per_peer
        == lax.broadcasted_iota(jnp.int32, (bound, per_peer), 1)
    )
    own_hub = (
        lax.broadcasted_iota(jnp.int32, (2 * hubs, hubs), 0) % hubs
        == lax.broadcasted_iota(jnp.int32, (2 * hubs, hubs), 1)
    )
    spread_hubs = jnp.broadcast_to(hubs_ref[...], (2 * hubs, hubs))

    def digit(take):
        sent = take(lists_ref[...]).astype(F32).astype(BF16)
        rows = jnp.sum(jnp.where(own_slot, dot(owner, sent, 1, 1), 0.0), axis=1, keepdims=True)
        hub = jnp.sum(
            jnp.where(own_hub, take(spread_hubs).astype(F32), 0.0), axis=1, keepdims=True
        )
        column = jnp.concatenate([rows, hub], axis=0)
        return jnp.broadcast_to(column, (bound + 2 * hubs, LO)).astype(BF16)

    list_high, list_low = digit(lambda v: v >> 8), digit(lambda v: v & (LO - 1))
    lane = lax.broadcasted_iota(jnp.int32, (bound + 2 * hubs, LO), 1).astype(F32).astype(BF16)
    for h in range(nodes // LO):
        low = jnp.where(list_high == jnp.full((), h, BF16), list_low, -one)
        picks[:, h * LO : (h + 1) * LO] = jnp.where(low == lane, one, zero)
    loads[2].wait()
    packed = dot(picks[...], features_ref[...], 1, 0)
    hub_tile = halves(packed[bound : bound + hubs])
    rows_send[...] = jnp.concatenate(
        [halves(packed[:bound]), jnp.broadcast_to(hub_tile, (peers, 16, LANES))], axis=1
    ).astype(BF16)
    rows_in[me] = rows_send[me]
    picks_copy = pltpu.make_async_copy(picks, picks_out, out_sem.at[1])
    picks_copy.start()
    pl.semaphore_wait(barrier, peers - 1)

    @pl.loop(1, peers)
    def _(p):
        peer = lax.rem(me + p, peers)
        pltpu.make_async_remote_copy(
            src_ref=rows_send.at[peer], dst_ref=rows_in.at[me],
            send_sem=row_sem.at[0], recv_sem=row_sem.at[1],
            device_id=(peer,), device_id_type=MESH,
        ).start()

    loads[3].wait()
    loads[4].wait()
    usable = lax.broadcasted_iota(jnp.int32, (fan, nodes), 0) < counts_ref[...]
    index = jnp.where(usable, index_ref[...], -1)
    stacked = jnp.concatenate(
        [index[:, j * groups : (j + 1) * groups] for j in range(GROUP)], axis=0
    )
    high_rows[...] = (stacked >> 8).astype(F32).T
    low_rows[...] = (stacked & (LO - 1)).astype(F32).T
    pairs = GROUP * fan
    mine = (
        lax.broadcasted_iota(jnp.int32, (GROUP, pairs), 0)
        == lax.broadcasted_iota(jnp.int32, (GROUP, pairs), 1) // fan
    )
    low_ids = lax.broadcasted_iota(jnp.int32, (LO, pairs), 0).astype(F32).astype(BF16)

    @pl.loop(0, groups // 16)
    def _(step):
        at16 = pl.ds(pl.multiple_of(step * 16, 16), 16)
        highs, lows = high_rows[at16, :], low_rows[at16, :]
        for group in range(16):
            high = jnp.broadcast_to(highs[group : group + 1, :], (GROUP, pairs)).astype(BF16)
            high = jnp.where(mine, high, -one)
            low = jnp.broadcast_to(lows[group : group + 1, :], (16, pairs)).astype(BF16)
            low = jnp.concatenate([low] * (LO // 16), axis=0)
            low_hot = jnp.where(low_ids == low, one, zero).astype(F8)
            high_hot = jnp.concatenate(
                [jnp.where(high == jnp.full((), h, BF16), one, zero) for h in range(blocks)],
                axis=0,
            ).astype(F8)
            counted = dot(high_hot, low_hot, 1, 1).astype(BF16)
            at = pl.ds(pl.multiple_of(step * 256 + 16 * group, 16), 16)
            for h in range(blocks):
                count[at, h * LO : (h + 1) * LO] = counted[16 * h : 16 * h + 16]

    total = dot(count[:, :nodes], features_ref[...], 1, 0)
    for i in range(width // LANES):
        summed[i] = total[:, i * LANES : (i + 1) * LANES]

    others = pl.ds(0, peers - 1)
    pltpu.make_async_copy(rows_in.at[others], rows_in.at[others], row_sem.at[1]).wait()
    arrived = rows_in[...].astype(F32)
    table = jnp.concatenate([joined(arrived[:, :16]), joined(arrived[:, 16:])], axis=0)
    total = dot(count[:, nodes:], table.astype(BF16), 1, 0)
    for i in range(width // LANES):
        summed[i] = summed[i] + total[:, i * LANES : (i + 1) * LANES]

    for load in loads[5:]:
        load.wait()
    inverse = 1.0 / counts_ref[...].astype(F32)
    columns = []
    for j in range(GROUP):
        at = slice(j * groups, (j + 1) * groups)
        column = jnp.broadcast_to(inverse[:, at], (LANES, groups)).T
        columns.append(column)
        strided = pl.ds(j, groups, stride=GROUP)
        mean_all[at, :] = jnp.concatenate(
            [summed[i, strided, :] * column for i in range(width // LANES)], axis=1
        ).astype(BF16)
    pre = dot(features_ref[...], self_ref[...], 1, 0) + dot(mean_all[...], neighbour_ref[...], 1, 0)
    sig = jax.nn.sigmoid(pre)
    activations_ref[...] = (pre * sig).astype(BF16)
    grad_pre = (
        cotangent_ref[...].astype(F32) * sig * (1.0 + pre * (1.0 - sig))
    ).astype(BF16)
    grad_t[...] = grad_pre.T
    act_copy = pltpu.make_async_copy(activations_ref, activations_out, out_sem.at[0])
    act_copy.start()

    upper = dot(grad_t[...], features_ref[...], 1, 0).T
    lower = dot(grad_t[...], mean_all[...], 1, 0).T
    for o in range(peers):
        source = upper if o * share < width else lower
        start = o * share % width
        for i in range(width // LANES):
            pair_send[o % 2, (o // 2) % inner, o // (2 * inner), i * share : (i + 1) * share] = (
                source[start : start + share, i * LANES : (i + 1) * LANES]
            )

    def to_pair(source, target, sem):
        return pltpu.make_async_remote_copy(
            src_ref=source.at[1 - core], dst_ref=target,
            send_sem=sem.at[0], recv_sem=sem.at[1],
            device_id=(me + 1 - 2 * core,), device_id_type=MESH,
        )

    def to_inner(source, target, sem):
        @pl.loop(1, inner)
        def _(p):
            to = lax.rem(my_inner + p, inner)
            pltpu.make_async_remote_copy(
                src_ref=source.at[to], dst_ref=target.at[my_inner],
                send_sem=sem.at[0], recv_sem=sem.at[1],
                device_id=((my_outer * inner + to) * 2 + core,), device_id_type=MESH,
            ).start()

    def wait_for(ref, amount, sem):
        part = ref.at[pl.ds(0, amount)]
        pltpu.make_async_copy(part, part, sem).wait()

    pair_copy = to_pair(pair_send, pair_in, pair_sem)
    pair_copy.start()

    edge = dot(grad_pre, neighbour_ref[...], 1, 1)
    for j in range(GROUP):
        at = slice(j * groups, (j + 1) * groups)
        strided = pl.ds(j, groups, stride=GROUP)
        for i in range(width // LANES):
            edge_rows[i, strided, :] = edge[at, i * LANES : (i + 1) * LANES] * columns[j]
    for i in range(width // LANES):
        edge_t[i * LANES : (i + 1) * LANES, :] = edge_rows[i].astype(BF16).T

    pair_copy.wait_recv()
    inner_send[...] = (pair_send[core] + pair_in[...]).astype(BF16)
    own_inner = pair_send[core, my_inner] + pair_in[my_inner]
    to_inner(inner_send, inner_in, inner_sem)

    part = halves(dot(edge_t[...], count[:, nodes:], 1, 0).T)
    for o in range(peers):
        hub_pair_send[o % 2, (o // 2) % inner, o // (2 * inner)] = part[peers + o]
    hub_pair_copy = to_pair(hub_pair_send, hub_pair_in, hub_pair_sem)
    hub_pair_copy.start()
    part_send[...] = part[:peers].astype(BF16)
    part_in[me] = part_send[me]

    @pl.loop(1, peers)
    def _(p):
        peer = lax.rem(me + p, peers)
        pltpu.make_async_remote_copy(
            src_ref=part_send.at[peer], dst_ref=part_in.at[me],
            send_sem=part_sem.at[0], recv_sem=part_sem.at[1],
            device_id=(peer,), device_id_type=MESH,
        ).start()

    hub_pair_copy.wait_recv()
    hub_inner_send[...] = (hub_pair_send[core] + hub_pair_in[...]).astype(BF16)
    own_hub_inner = hub_pair_send[core, my_inner] + hub_pair_in[my_inner]
    to_inner(hub_inner_send, hub_inner_in, hub_inner_sem)

    def local(first, last):
        at = slice(first * LO, last * LO)
        part = dot(edge_t[...], count[:, at], 1, 0) + dot(self_ref[...], grad_t[:, at], 1, 0)
        base[at, :] = part.T
        pltpu.make_async_copy(base.at[at], base_out.at[at], out_sem.at[2]).start()

    local_blocks = nodes // LO
    local(0, local_blocks // 2)

    inner_in[my_inner] = jnp.zeros(inner_in.shape[1:], BF16)
    hub_inner_in[my_inner] = jnp.zeros(hub_inner_in.shape[1:], BF16)
    wait_for(inner_in, inner - 1, inner_sem.at[1])
    wait_for(hub_inner_in, inner - 1, hub_inner_sem.at[1])
    weights_at, hubs_at = slice(0, 2 * share), slice(2 * share, 2 * share + 16)
    pair_in[0] = own_inner + jnp.sum(inner_in[...].astype(F32), axis=0)
    hub_pair_in[0] = own_hub_inner + jnp.sum(hub_inner_in[...].astype(F32), axis=0)
    outer_send[:, weights_at] = pair_in[0].astype(BF16)
    outer_send[:, hubs_at] = hub_pair_in[0].astype(BF16)

    @pl.loop(1, outer)
    def _(p):
        to = lax.rem(my_outer + p, outer)
        pltpu.make_async_remote_copy(
            src_ref=outer_send.at[to], dst_ref=outer_in.at[my_outer],
            send_sem=outer_sem.at[0], recv_sem=outer_sem.at[1],
            device_id=((to * inner + my_inner) * 2 + core,), device_id_type=MESH,
        ).start()

    local(local_blocks // 2, local_blocks)

    outer_in[my_outer] = jnp.zeros(outer_in.shape[1:], BF16)
    wait_for(part_in, peers - 1, part_sem.at[1])
    wait_for(outer_in, outer - 1, outer_sem.at[1])
    arrived = jnp.sum(outer_in[...].astype(F32), axis=0)
    weights = pair_in[0, my_outer] + arrived[weights_at]
    for i in range(width // LANES):
        weight_sum[:, i * LANES : (i + 1) * LANES] = weights[i * share : (i + 1) * share]
    hub_sum = joined((hub_pair_in[0, my_outer] + arrived[hubs_at])[None])
    hub_high = hub_sum.astype(BF16).astype(F32)
    returned_t[...] = jnp.concatenate(
        [joined(part_in[...].astype(F32)), hub_high, hub_sum - hub_high], axis=0
    ).astype(BF16).T
    last = (
        pltpu.make_async_copy(returned_t, returned_out, out_sem.at[3]),
        pltpu.make_async_copy(weight_sum, weight_out, out_sem.at[4]),
    )
    for copy in last:
        copy.start()

    wait_for(rows_send, peers - 1, row_sem.at[0])
    wait_for(part_send, peers - 1, part_sem.at[0])
    pair_copy.wait_send()
    hub_pair_copy.wait_send()
    wait_for(inner_send, inner - 1, inner_sem.at[0])
    wait_for(hub_inner_send, inner - 1, hub_inner_sem.at[0])
    wait_for(outer_send, outer - 1, outer_sem.at[0])
    act_copy.wait()
    picks_copy.wait()
    pltpu.make_async_copy(base, base_out, out_sem.at[2]).wait()
    for copy in last:
        copy.wait()


def finish_kernel(
    activations_in, base_in, picks_in, returned_in, weights_in,
    activations_out, grads_out, weights_out,
    picks, returned_t, base, activations, weights, in_sem, out_sem,
):
    nodes = base.shape[0]
    step = nodes // FINISH_STEPS
    slices = [slice(start, start + step) for start in range(0, nodes, step)]
    returned_read = pltpu.make_async_copy(returned_in, returned_t, in_sem.at[0])
    reads = [
        (
            pltpu.make_async_copy(picks_in.at[:, at], picks.at[:, at], in_sem.at[3 + 2 * i]),
            pltpu.make_async_copy(base_in.at[at], base.at[at], in_sem.at[4 + 2 * i]),
        )
        for i, at in enumerate(slices)
    ]
    through = (
        pltpu.make_async_copy(activations_in, activations, in_sem.at[1]),
        pltpu.make_async_copy(weights_in, weights, in_sem.at[2]),
    )
    writes = (
        pltpu.make_async_copy(activations, activations_out, out_sem.at[0]),
        pltpu.make_async_copy(weights, weights_out, out_sem.at[1]),
    )
    for read in (returned_read,) + reads[0] + through + sum(reads[1:], ()):
        read.start()
    returned_read.wait()
    for i, at in enumerate(slices):
        for read in reads[i]:
            read.wait()
        base[at, :] = base[at, :] + dot(returned_t[...], picks[:, at], 1, 0).T
        pltpu.make_async_copy(base.at[at], grads_out.at[at], out_sem.at[2]).start()
        if i == 0:
            for read, write in zip(through, writes):
                read.wait()
                write.start()
    for write in writes:
        write.wait()
    pltpu.make_async_copy(base, grads_out, out_sem.at[2]).wait()


def body(
    features, self_weight, neighbour_weight, send_lists, hub_nodes, neighbours, counts, cotangent
):
    nodes, width = features.shape
    fan = neighbours.shape[1]
    peers = lax.axis_size("dom")
    per_peer = send_lists.shape[2]
    hubs = hub_nodes.shape[1]
    bound = peers * per_peer
    columns = nodes + bound + peers * hubs
    share = 2 * width // peers
    outer, inner = split(peers)
    dma = pltpu.SemaphoreType.DMA
    any_space = pl.BlockSpec(memory_space=pl.ANY)
    picked = bound + 2 * hubs
    activations, base, picks, returned, weights = pl.pallas_call(
        functools.partial(whole_kernel, peers),
        in_specs=[any_space] * 8,
        out_specs=[any_space] * 5,
        out_shape=[
            jax.ShapeDtypeStruct((nodes, width), BF16),
            jax.ShapeDtypeStruct((nodes, width), F32),
            jax.ShapeDtypeStruct((picked, nodes), BF16),
            jax.ShapeDtypeStruct((width, picked), BF16),
            jax.ShapeDtypeStruct((share, width), F32),
        ],
        scratch_shapes=[
            pltpu.VMEM((fan, nodes), jnp.int32),
            pltpu.VMEM((1, nodes), jnp.int32),
            pltpu.VMEM((per_peer, peers), jnp.int32),
            pltpu.VMEM((1, hubs), jnp.int32),
            pltpu.VMEM((nodes, width), BF16),
            pltpu.VMEM((nodes, width), BF16),
            pltpu.VMEM((width, width), BF16),
            pltpu.VMEM((width, width), BF16),
            pltpu.VMEM((picked, nodes), BF16),
            pltpu.VMEM((peers, 32, LANES), BF16),
            pltpu.VMEM((peers, 32, LANES), BF16),
            pltpu.VMEM((nodes // GROUP, GROUP * fan), F32),
            pltpu.VMEM((nodes // GROUP, GROUP * fan), F32),
            pltpu.VMEM((nodes, columns), BF16),
            pltpu.VMEM((width // LANES, nodes, LANES), F32),
            pltpu.VMEM((nodes, width), BF16),
            pltpu.VMEM((width, nodes), BF16),
            pltpu.VMEM((width // LANES, nodes, LANES), F32),
            pltpu.VMEM((width, nodes), BF16),
            pltpu.VMEM((nodes, width), BF16),
            pltpu.VMEM((nodes, width), F32),
            pltpu.VMEM((width, picked), BF16),
            pltpu.VMEM((share, width), F32),
            pltpu.VMEM((peers, 16, LANES), BF16),
            pltpu.VMEM((peers, 16, LANES), BF16),
            pltpu.VMEM((2, inner, outer, 2 * share, LANES), F32),
            pltpu.VMEM((inner, outer, 2 * share, LANES), F32),
            pltpu.VMEM((inner, outer, 2 * share, LANES), BF16),
            pltpu.VMEM((inner, outer, 2 * share, LANES), BF16),
            pltpu.VMEM((2, inner, outer, 16, LANES), F32),
            pltpu.VMEM((inner, outer, 16, LANES), F32),
            pltpu.VMEM((inner, outer, 16, LANES), BF16),
            pltpu.VMEM((inner, outer, 16, LANES), BF16),
            pltpu.VMEM((outer, 2 * share + 16, LANES), BF16),
            pltpu.VMEM((outer, 2 * share + 16, LANES), BF16),
            dma((8,)), dma((2,)), dma((2,)), dma((2,)), dma((2,)), dma((2,)), dma((2,)), dma((2,)),
            dma((5,)),
        ],
        compiler_params=pltpu.CompilerParams(
            collective_id=0, has_side_effects=True, vmem_limit_bytes=VMEM_MAIN * 1024 * 1024
        ),
        name="whole",
    )(
        neighbours.T, counts[None, :], send_lists[0].T, hub_nodes, features, cotangent, self_weight,
        neighbour_weight,
    )
    return pl.pallas_call(
        finish_kernel,
        in_specs=[any_space] * 5,
        out_specs=[any_space] * 3,
        out_shape=[
            jax.ShapeDtypeStruct((nodes, width), BF16),
            jax.ShapeDtypeStruct((nodes, width), F32),
            jax.ShapeDtypeStruct((share, width), F32),
        ],
        scratch_shapes=[
            pltpu.VMEM((picked, nodes), BF16),
            pltpu.VMEM((width, picked), BF16),
            pltpu.VMEM((nodes, width), F32),
            pltpu.VMEM((nodes, width), BF16),
            pltpu.VMEM((share, width), F32),
            dma((3 + 2 * FINISH_STEPS,)), dma((3,)),
        ],
        compiler_params=pltpu.CompilerParams(vmem_limit_bytes=60 * 1024 * 1024),
        name="finish",
    )(activations, base, picks, returned, weights)


def solution(mesh):
    in_specs = (
        P("dom", None),
        P(),
        P(),
        P("dom", None, None),
        P("dom", None),
        P("dom", None),
        P("dom"),
        P("dom", None),
    )
    out_specs = (P("dom", None), P("dom", None), P("dom", None))
    return jax.shard_map(body, mesh=mesh, in_specs=in_specs, out_specs=out_specs, check_vma=False)
```

```python
import functools

import jax
import jax.numpy as jnp
from jax import lax
from jax.experimental import pallas as pl
from jax.experimental.pallas import tpu as pltpu
from jax.sharding import PartitionSpec as P

LO = 256
LANES = 128
VMEM_MAIN = 60
FINISH_STEPS = 4
GROUP = 16
BF16 = jnp.bfloat16
F32 = jnp.float32
F8 = jnp.float8_e4m3fn
MESH = pl.DeviceIdType.MESH


def dot(a, b, ca, cb):
    return lax.dot_general(a, b, (((ca,), (cb,)), ((), ())), preferred_element_type=F32)


def split(peers):
    half = peers // 2
    inner = 1
    while inner * inner < half:
        inner *= 2
    return half // inner, inner


def halves(rows):
    count, width = rows.shape[0] // 8, rows.shape[1] // LANES
    return jnp.concatenate(
        [rows[:, i * LANES : (i + 1) * LANES].reshape(count, 8, LANES) for i in range(width)], axis=1
    )


def joined(tiles):
    count, width = tiles.shape[0], tiles.shape[1] // 8
    return jnp.concatenate(
        [tiles[:, i * 8 : (i + 1) * 8].reshape(count * 8, LANES) for i in range(width)], axis=1
    )


def whole_kernel(
    peers,
    neighbours_in, counts_in, lists_in, hubs_in, features_in, cotangent_in, self_in, neighbour_in,
    activations_out, base_out, picks_out, returned_out, weight_out,
    index_ref, counts_ref, lists_ref, hubs_ref, features_ref, cotangent_ref, self_ref, neighbour_ref,
    picks, rows_send, rows_in, spread_rows, high_rows, low_rows, count, summed, mean_all, grad_t, edge_t,
    activations_ref, base, returned_t, weight_sum, part_send, part_in,
    pair_send, pair_in, inner_send, inner_in, hub_pair_send, hub_pair_in, hub_send, hub_in,
    outer_send, outer_in,
    in_sem, row_sem, part_sem, pair_sem, inner_sem, hub_pair_sem, hub_sem, outer_sem, out_sem,
):
    me = lax.axis_index("dom")
    outer, inner = split(peers)
    core = me % 2
    my_inner = (me // 2) % inner
    my_outer = me // (2 * inner)
    half, my_half = outer * inner, me // 2
    nodes, width = features_ref.shape
    fan = index_ref.shape[0]
    per_peer = lists_ref.shape[0]
    hubs = hubs_ref.shape[1]
    bound = peers * per_peer
    groups = nodes // GROUP
    blocks = count.shape[1] // LO
    share = weight_sum.shape[0]

    ins = (
        (lists_in, lists_ref), (hubs_in, hubs_ref), (features_in, features_ref),
        (neighbours_in, index_ref), (counts_in, counts_ref), (self_in, self_ref),
        (neighbour_in, neighbour_ref), (cotangent_in, cotangent_ref),
    )
    loads = [pltpu.make_async_copy(a, b, in_sem.at[i]) for i, (a, b) in enumerate(ins)]
    for load in loads:
        load.start()

    barrier = pltpu.get_barrier_semaphore()

    @pl.loop(1, peers)
    def _(p):
        pl.semaphore_signal(
            barrier, inc=1, device_id=(lax.rem(me + p, peers),), device_id_type=MESH
        )

    one = jnp.ones((), BF16)
    zero = jnp.zeros((), BF16)

    loads[0].wait()
    loads[1].wait()
    owner = jnp.where(
        lax.broadcasted_iota(jnp.int32, (bound, peers), 0) // per_peer
        == lax.broadcasted_iota(jnp.int32, (bound, peers), 1), 1.0, 0.0,
    ).astype(BF16)
    own_slot = (
        lax.broadcasted_iota(jnp.int32, (bound, per_peer), 0) % per_peer
        == lax.broadcasted_iota(jnp.int32, (bound, per_peer), 1)
    )
    own_hub = (
        lax.broadcasted_iota(jnp.int32, (2 * hubs, hubs), 0) % hubs
        == lax.broadcasted_iota(jnp.int32, (2 * hubs, hubs), 1)
    )
    spread_hubs = jnp.broadcast_to(hubs_ref[...], (2 * hubs, hubs))

    def digit(take):
        sent = take(lists_ref[...]).astype(F32).astype(BF16)
        rows = jnp.sum(jnp.where(own_slot, dot(owner, sent, 1, 1), 0.0), axis=1, keepdims=True)
        hub = jnp.sum(
            jnp.where(own_hub, take(spread_hubs).astype(F32), 0.0), axis=1, keepdims=True
        )
        column = jnp.concatenate([rows, hub], axis=0)
        return jnp.broadcast_to(column, (bound + 2 * hubs, LO)).astype(BF16)

    list_high, list_low = digit(lambda v: v >> 8), digit(lambda v: v & (LO - 1))
    lane = lax.broadcasted_iota(jnp.int32, (bound + 2 * hubs, LO), 1).astype(F32).astype(BF16)
    for h in range(nodes // LO):
        low = jnp.where(list_high == jnp.full((), h, BF16), list_low, -one)
        picks[:, h * LO : (h + 1) * LO] = jnp.where(low == lane, one, zero)
    loads[2].wait()
    packed = dot(picks[...], features_ref[...], 1, 0)
    hub_tile = halves(packed[bound : bound + hubs])
    rows_send[...] = jnp.concatenate(
        [halves(packed[:bound]), jnp.broadcast_to(hub_tile, (peers, 16, LANES))], axis=1
    ).astype(BF16)
    rows_in[me] = rows_send[me]
    picks_copy = pltpu.make_async_copy(picks, picks_out, out_sem.at[1])
    picks_copy.start()
    pl.semaphore_wait(barrier, peers - 1)

    @pl.loop(1, peers)
    def _(p):
        peer = lax.rem(me + p, peers)
        pltpu.make_async_remote_copy(
            src_ref=rows_send.at[peer], dst_ref=rows_in.at[me],
            send_sem=row_sem.at[0], recv_sem=row_sem.at[1],
            device_id=(peer,), device_id_type=MESH,
        ).start()

    loads[3].wait()
    loads[4].wait()
    usable = lax.broadcasted_iota(jnp.int32, (fan, nodes), 0) < counts_ref[...]
    index = jnp.where(usable, index_ref[...], -1).astype(F32)
    for start in range(0, nodes, LANES):
        spread = jnp.concatenate([index[:, start : start + LANES]] * (LANES // fan), axis=0)
        spread_rows[start : start + LANES, :] = spread.T
    slot_of = lax.broadcasted_iota(jnp.int32, (groups, LANES), 1) // fan
    tiles = []
    for first in range(0, GROUP, LANES // fan):
        tile = spread_rows[pl.ds(first, groups, stride=GROUP), :]
        for j in range(1, LANES // fan):
            piece = spread_rows[pl.ds(first + j, groups, stride=GROUP), :]
            tile = jnp.where(slot_of == j, piece, tile)
        tiles.append(tile)
    grouped = jnp.concatenate(tiles, axis=1).astype(jnp.int32)
    high_rows[...] = (grouped >> 8).astype(F32)
    low_rows[...] = (grouped & (LO - 1)).astype(F32)
    pairs = GROUP * fan
    mine = (
        lax.broadcasted_iota(jnp.int32, (GROUP, pairs), 0)
        == lax.broadcasted_iota(jnp.int32, (GROUP, pairs), 1) // fan
    )
    low_ids = lax.broadcasted_iota(jnp.int32, (LO, pairs), 0).astype(F32).astype(BF16)

    @pl.loop(0, groups // 16)
    def _(step):
        at16 = pl.ds(pl.multiple_of(step * 16, 16), 16)
        highs, lows = high_rows[at16, :], low_rows[at16, :]
        for group in range(16):
            high = jnp.broadcast_to(highs[group : group + 1, :], (GROUP, pairs)).astype(BF16)
            high = jnp.where(mine, high, -one)
            low = jnp.broadcast_to(lows[group : group + 1, :], (16, pairs)).astype(BF16)
            low = jnp.concatenate([low] * (LO // 16), axis=0)
            low_hot = jnp.where(low_ids == low, one, zero).astype(F8)
            high_hot = jnp.concatenate(
                [jnp.where(high == jnp.full((), h, BF16), one, zero) for h in range(blocks)],
                axis=0,
            ).astype(F8)
            counted = dot(high_hot, low_hot, 1, 1).astype(BF16)
            at = pl.ds(pl.multiple_of(step * 256 + 16 * group, 16), 16)
            for h in range(blocks):
                count[at, h * LO : (h + 1) * LO] = counted[16 * h : 16 * h + 16]

    summed[...] = dot(count[:, :nodes], features_ref[...], 1, 0)

    others = pl.ds(0, peers - 1)
    pltpu.make_async_copy(rows_in.at[others], rows_in.at[others], row_sem.at[1]).wait()
    arrived = rows_in[...].astype(F32)
    table = jnp.concatenate([joined(arrived[:, :16]), joined(arrived[:, 16:])], axis=0)
    total = summed[...] + dot(count[:, nodes:], table.astype(BF16), 1, 0)

    for load in loads[5:]:
        load.wait()
    inverse = 1.0 / counts_ref[...].astype(F32)
    column = jnp.concatenate(
        [
            jnp.broadcast_to(inverse[:, start : start + LANES], (LANES, LANES)).T
            for start in range(0, nodes, LANES)
        ],
        axis=0,
    )
    mean_all[...] = jnp.concatenate(
        [total[:, start : start + LANES] * column for start in range(0, width, LANES)], axis=1
    ).astype(BF16)
    pre = dot(features_ref[...], self_ref[...], 1, 0) + dot(mean_all[...], neighbour_ref[...], 1, 0)
    sig = jax.nn.sigmoid(pre)
    activations_ref[...] = (pre * sig).astype(BF16)
    grad_pre = (
        cotangent_ref[...].astype(F32) * sig * (1.0 + pre * (1.0 - sig))
    ).astype(BF16)
    grad_t[...] = grad_pre.T
    act_copy = pltpu.make_async_copy(activations_ref, activations_out, out_sem.at[0])
    act_copy.start()

    upper = dot(grad_t[...], features_ref[...], 1, 0).T
    lower = dot(grad_t[...], mean_all[...], 1, 0).T
    for o in range(peers):
        source = upper if o * share < width else lower
        start = o * share % width
        for i in range(width // LANES):
            pair_send[o % 2, (o // 2) % inner, o // (2 * inner), i * share : (i + 1) * share] = (
                source[start : start + share, i * LANES : (i + 1) * LANES]
            )

    def to_pair(source, target, sem):
        return pltpu.make_async_remote_copy(
            src_ref=source.at[1 - core], dst_ref=target,
            send_sem=sem.at[0], recv_sem=sem.at[1],
            device_id=(me + 1 - 2 * core,), device_id_type=MESH,
        )

    def to_inner(source, target, sem):
        @pl.loop(1, inner)
        def _(p):
            to = lax.rem(my_inner + p, inner)
            pltpu.make_async_remote_copy(
                src_ref=source.at[to], dst_ref=target.at[my_inner],
                send_sem=sem.at[0], recv_sem=sem.at[1],
                device_id=((my_outer * inner + to) * 2 + core,), device_id_type=MESH,
            ).start()

    def wait_for(ref, amount, sem):
        part = ref.at[pl.ds(0, amount)]
        pltpu.make_async_copy(part, part, sem).wait()

    pair_copy = to_pair(pair_send, pair_in, pair_sem)
    pair_copy.start()

    edge_t[...] = (dot(neighbour_ref[...], grad_t[...], 1, 0) * inverse).astype(BF16)

    pair_copy.wait_recv()
    inner_send[...] = (pair_send[core] + pair_in[...]).astype(BF16)
    own_inner = pair_send[core, my_inner] + pair_in[my_inner]
    to_inner(inner_send, inner_in, inner_sem)

    part = halves(dot(edge_t[...], count[:, nodes:], 1, 0).T)
    for o in range(peers):
        hub_pair_send[o % 2, (o // 2) % inner, o // (2 * inner)] = part[peers + o]
    hub_pair_copy = to_pair(hub_pair_send, hub_pair_in, hub_pair_sem)
    hub_pair_copy.start()
    part_send[...] = part[:peers].astype(BF16)
    part_in[me] = part_send[me]

    @pl.loop(1, peers)
    def _(p):
        peer = lax.rem(me + p, peers)
        pltpu.make_async_remote_copy(
            src_ref=part_send.at[peer], dst_ref=part_in.at[me],
            send_sem=part_sem.at[0], recv_sem=part_sem.at[1],
            device_id=(peer,), device_id_type=MESH,
        ).start()

    def local(first, last):
        at = slice(first * LO, last * LO)
        part = dot(edge_t[...], count[:, at], 1, 0) + dot(self_ref[...], grad_t[:, at], 1, 0)
        base[at, :] = part.T
        pltpu.make_async_copy(base.at[at], base_out.at[at], out_sem.at[2]).start()

    local_blocks = nodes // LO
    local(0, local_blocks // 4)

    hub_pair_copy.wait_recv()
    hub_send[...] = (hub_pair_send[core] + hub_pair_in[...]).astype(BF16)

    @pl.loop(1, half)
    def _(p):
        to = lax.rem(my_half + p, half)
        pltpu.make_async_remote_copy(
            src_ref=hub_send.at[lax.rem(to, inner), to // inner], dst_ref=hub_in.at[my_half],
            send_sem=hub_sem.at[0], recv_sem=hub_sem.at[1],
            device_id=(to * 2 + core,), device_id_type=MESH,
        ).start()

    inner_in[my_inner] = jnp.zeros(inner_in.shape[1:], BF16)
    wait_for(inner_in, inner - 1, inner_sem.at[1])
    pair_in[0] = own_inner + jnp.sum(inner_in[...].astype(F32), axis=0)
    outer_send[...] = pair_in[0].astype(BF16)

    @pl.loop(1, outer)
    def _(p):
        to = lax.rem(my_outer + p, outer)
        pltpu.make_async_remote_copy(
            src_ref=outer_send.at[to], dst_ref=outer_in.at[my_outer],
            send_sem=outer_sem.at[0], recv_sem=outer_sem.at[1],
            device_id=((to * inner + my_inner) * 2 + core,), device_id_type=MESH,
        ).start()

    local(local_blocks // 4, local_blocks)

    outer_in[my_outer] = jnp.zeros(outer_in.shape[1:], BF16)
    wait_for(part_in, peers - 1, part_sem.at[1])
    wait_for(outer_in, outer - 1, outer_sem.at[1])
    weights = pair_in[0, my_outer] + jnp.sum(outer_in[...].astype(F32), axis=0)
    for i in range(width // LANES):
        weight_sum[:, i * LANES : (i + 1) * LANES] = weights[i * share : (i + 1) * share]
    hub_in[my_half] = jnp.zeros(hub_in.shape[1:], BF16)
    wait_for(hub_in, half - 1, hub_sem.at[1])
    own_hub = hub_pair_send[core, my_inner, my_outer] + hub_pair_in[my_inner, my_outer]
    hub_sum = joined((own_hub + jnp.sum(hub_in[...].astype(F32), axis=0))[None])
    hub_high = hub_sum.astype(BF16).astype(F32)
    returned_t[...] = jnp.concatenate(
        [joined(part_in[...].astype(F32)), hub_high, hub_sum - hub_high], axis=0
    ).astype(BF16).T
    last = (
        pltpu.make_async_copy(returned_t, returned_out, out_sem.at[3]),
        pltpu.make_async_copy(weight_sum, weight_out, out_sem.at[4]),
    )
    for copy in last:
        copy.start()

    wait_for(rows_send, peers - 1, row_sem.at[0])
    wait_for(part_send, peers - 1, part_sem.at[0])
    pair_copy.wait_send()
    hub_pair_copy.wait_send()
    wait_for(inner_send, inner - 1, inner_sem.at[0])
    hub_sent = hub_in.at[pl.ds(0, half - 1)]
    pltpu.make_async_copy(hub_sent, hub_sent, hub_sem.at[0]).wait()
    wait_for(outer_send, outer - 1, outer_sem.at[0])
    act_copy.wait()
    picks_copy.wait()
    pltpu.make_async_copy(base, base_out, out_sem.at[2]).wait()
    for copy in last:
        copy.wait()


def finish_kernel(
    activations_in, base_in, picks_in, returned_in, weights_in,
    activations_out, grads_out, weights_out,
    picks, returned_t, base, activations, weights, in_sem, out_sem,
):
    nodes = base.shape[0]
    step = nodes // FINISH_STEPS
    slices = [slice(start, start + step) for start in range(0, nodes, step)]
    returned_read = pltpu.make_async_copy(returned_in, returned_t, in_sem.at[0])
    reads = [
        (
            pltpu.make_async_copy(picks_in.at[:, at], picks.at[:, at], in_sem.at[3 + 2 * i]),
            pltpu.make_async_copy(base_in.at[at], base.at[at], in_sem.at[4 + 2 * i]),
        )
        for i, at in enumerate(slices)
    ]
    through = (
        pltpu.make_async_copy(activations_in, activations, in_sem.at[1]),
        pltpu.make_async_copy(weights_in, weights, in_sem.at[2]),
    )
    writes = (
        pltpu.make_async_copy(activations, activations_out, out_sem.at[0]),
        pltpu.make_async_copy(weights, weights_out, out_sem.at[1]),
    )
    for read in (returned_read,) + reads[0] + through + sum(reads[1:], ()):
        read.start()
    returned_read.wait()
    for i, at in enumerate(slices):
        for read in reads[i]:
            read.wait()
        base[at, :] = base[at, :] + dot(returned_t[...], picks[:, at], 1, 0).T
        pltpu.make_async_copy(base.at[at], grads_out.at[at], out_sem.at[2]).start()
        if i == 0:
            for read, write in zip(through, writes):
                read.wait()
                write.start()
    for write in writes:
        write.wait()
    pltpu.make_async_copy(base, grads_out, out_sem.at[2]).wait()


def body(
    features, self_weight, neighbour_weight, send_lists, hub_nodes, neighbours, counts, cotangent
):
    nodes, width = features.shape
    fan = neighbours.shape[1]
    peers = lax.axis_size("dom")
    per_peer = send_lists.shape[2]
    hubs = hub_nodes.shape[1]
    bound = peers * per_peer
    columns = nodes + bound + peers * hubs
    share = 2 * width // peers
    outer, inner = split(peers)
    dma = pltpu.SemaphoreType.DMA
    any_space = pl.BlockSpec(memory_space=pl.ANY)
    picked = bound + 2 * hubs
    activations, base, picks, returned, weights = pl.pallas_call(
        functools.partial(whole_kernel, peers),
        in_specs=[any_space] * 8,
        out_specs=[any_space] * 5,
        out_shape=[
            jax.ShapeDtypeStruct((nodes, width), BF16),
            jax.ShapeDtypeStruct((nodes, width), F32),
            jax.ShapeDtypeStruct((picked, nodes), BF16),
            jax.ShapeDtypeStruct((width, picked), BF16),
            jax.ShapeDtypeStruct((share, width), F32),
        ],
        scratch_shapes=[
            pltpu.VMEM((fan, nodes), jnp.int32),
            pltpu.VMEM((1, nodes), jnp.int32),
            pltpu.VMEM((per_peer, peers), jnp.int32),
            pltpu.VMEM((1, hubs), jnp.int32),
            pltpu.VMEM((nodes, width), BF16),
            pltpu.VMEM((nodes, width), BF16),
            pltpu.VMEM((width, width), BF16),
            pltpu.VMEM((width, width), BF16),
            pltpu.VMEM((picked, nodes), BF16),
            pltpu.VMEM((peers, 32, LANES), BF16),
            pltpu.VMEM((peers, 32, LANES), BF16),
            pltpu.VMEM((nodes, LANES), F32),
            pltpu.VMEM((nodes // GROUP, GROUP * fan), F32),
            pltpu.VMEM((nodes // GROUP, GROUP * fan), F32),
            pltpu.VMEM((nodes, columns), BF16),
            pltpu.VMEM((nodes, width), F32),
            pltpu.VMEM((nodes, width), BF16),
            pltpu.VMEM((width, nodes), BF16),
            pltpu.VMEM((width, nodes), BF16),
            pltpu.VMEM((nodes, width), BF16),
            pltpu.VMEM((nodes, width), F32),
            pltpu.VMEM((width, picked), BF16),
            pltpu.VMEM((share, width), F32),
            pltpu.VMEM((peers, 16, LANES), BF16),
            pltpu.VMEM((peers, 16, LANES), BF16),
            pltpu.VMEM((2, inner, outer, 2 * share, LANES), F32),
            pltpu.VMEM((inner, outer, 2 * share, LANES), F32),
            pltpu.VMEM((inner, outer, 2 * share, LANES), BF16),
            pltpu.VMEM((inner, outer, 2 * share, LANES), BF16),
            pltpu.VMEM((2, inner, outer, 16, LANES), F32),
            pltpu.VMEM((inner, outer, 16, LANES), F32),
            pltpu.VMEM((inner, outer, 16, LANES), BF16),
            pltpu.VMEM((inner * outer, 16, LANES), BF16),
            pltpu.VMEM((outer, 2 * share, LANES), BF16),
            pltpu.VMEM((outer, 2 * share, LANES), BF16),
            dma((8,)), dma((2,)), dma((2,)), dma((2,)), dma((2,)), dma((2,)), dma((2,)), dma((2,)),
            dma((5,)),
        ],
        compiler_params=pltpu.CompilerParams(
            collective_id=0, has_side_effects=True, vmem_limit_bytes=VMEM_MAIN * 1024 * 1024
        ),
        name="whole",
    )(
        neighbours.T, counts[None, :], send_lists[0].T, hub_nodes, features, cotangent, self_weight,
        neighbour_weight,
    )
    return pl.pallas_call(
        finish_kernel,
        in_specs=[any_space] * 5,
        out_specs=[any_space] * 3,
        out_shape=[
            jax.ShapeDtypeStruct((nodes, width), BF16),
            jax.ShapeDtypeStruct((nodes, width), F32),
            jax.ShapeDtypeStruct((share, width), F32),
        ],
        scratch_shapes=[
            pltpu.VMEM((picked, nodes), BF16),
            pltpu.VMEM((width, picked), BF16),
            pltpu.VMEM((nodes, width), F32),
            pltpu.VMEM((nodes, width), BF16),
            pltpu.VMEM((share, width), F32),
            dma((3 + 2 * FINISH_STEPS,)), dma((3,)),
        ],
        compiler_params=pltpu.CompilerParams(vmem_limit_bytes=60 * 1024 * 1024),
        name="finish",
    )(activations, base, picks, returned, weights)


def solution(mesh):
    in_specs = (
        P("dom", None),
        P(),
        P(),
        P("dom", None, None),
        P("dom", None),
        P("dom", None),
        P("dom"),
        P("dom", None),
    )
    out_specs = (P("dom", None), P("dom", None), P("dom", None))
    return jax.shard_map(body, mesh=mesh, in_specs=in_specs, out_specs=out_specs, check_vma=False)
```

```python
import functools

import jax
import jax.numpy as jnp
from jax import lax
from jax.experimental import pallas as pl
from jax.experimental.pallas import tpu as pltpu
from jax.sharding import PartitionSpec as P

LO = 256
LANES = 128
VMEM_MAIN = 60
FINISH_STEPS = 4
GROUP = 16
UNROLL = 32
BF16 = jnp.bfloat16
F32 = jnp.float32
F8 = jnp.float8_e4m3fn
MESH = pl.DeviceIdType.MESH


def dot(a, b, ca, cb):
    return lax.dot_general(a, b, (((ca,), (cb,)), ((), ())), preferred_element_type=F32)


def halves(rows):
    count, width = rows.shape[0] // 8, rows.shape[1] // LANES
    return jnp.concatenate(
        [rows[:, i * LANES : (i + 1) * LANES].reshape(count, 8, LANES) for i in range(width)], axis=1
    )


def joined(tiles):
    count, width = tiles.shape[0], tiles.shape[1] // 8
    return jnp.concatenate(
        [tiles[:, i * 8 : (i + 1) * 8].reshape(count * 8, LANES) for i in range(width)], axis=1
    )


def whole_kernel(
    peers,
    neighbours_in, counts_in, lists_in, hubs_in, features_in, cotangent_in, self_in, neighbour_in,
    activations_out, base_out, picks_out, returned_out, weight_out,
    index_ref, counts_ref, lists_ref, hubs_ref, features_ref, cotangent_ref, self_ref, neighbour_ref,
    picks, rows_send, rows_in, spread_rows, high_rows, low_rows, count, summed, mean_all, grad_t, edge_t,
    activations_ref, base, returned_t, weight_sum, part_send, part_in,
    pair_send, pair_in, half_send, half_in, hub_pair_send, hub_pair_in, hub_send, hub_in,
    in_sem, row_sem, part_sem, pair_sem, half_sem, hub_pair_sem, hub_sem, out_sem,
):
    me = lax.axis_index("dom")
    core = me % 2
    half, my_half = peers // 2, me // 2
    nodes, width = features_ref.shape
    fan = index_ref.shape[0]
    per_peer = lists_ref.shape[0]
    hubs = hubs_ref.shape[1]
    bound = peers * per_peer
    groups = nodes // GROUP
    blocks = count.shape[1] // LO
    share = weight_sum.shape[0]

    ins = (
        (lists_in, lists_ref), (hubs_in, hubs_ref), (features_in, features_ref),
        (neighbours_in, index_ref), (counts_in, counts_ref), (self_in, self_ref),
        (neighbour_in, neighbour_ref), (cotangent_in, cotangent_ref),
    )
    loads = [pltpu.make_async_copy(a, b, in_sem.at[i]) for i, (a, b) in enumerate(ins)]
    for load in loads:
        load.start()

    barrier = pltpu.get_barrier_semaphore()

    @pl.loop(1, peers)
    def _(p):
        pl.semaphore_signal(
            barrier, inc=1, device_id=(lax.rem(me + p, peers),), device_id_type=MESH
        )

    one = jnp.ones((), BF16)
    zero = jnp.zeros((), BF16)

    loads[0].wait()
    loads[1].wait()
    owner = jnp.where(
        lax.broadcasted_iota(jnp.int32, (bound, peers), 0) // per_peer
        == lax.broadcasted_iota(jnp.int32, (bound, peers), 1), 1.0, 0.0,
    ).astype(BF16)
    own_slot = (
        lax.broadcasted_iota(jnp.int32, (bound, per_peer), 0) % per_peer
        == lax.broadcasted_iota(jnp.int32, (bound, per_peer), 1)
    )
    own_hub = (
        lax.broadcasted_iota(jnp.int32, (2 * hubs, hubs), 0) % hubs
        == lax.broadcasted_iota(jnp.int32, (2 * hubs, hubs), 1)
    )
    spread_hubs = jnp.broadcast_to(hubs_ref[...], (2 * hubs, hubs))

    def digit(take):
        sent = take(lists_ref[...]).astype(F32).astype(BF16)
        rows = jnp.sum(jnp.where(own_slot, dot(owner, sent, 1, 1), 0.0), axis=1, keepdims=True)
        hub = jnp.sum(
            jnp.where(own_hub, take(spread_hubs).astype(F32), 0.0), axis=1, keepdims=True
        )
        column = jnp.concatenate([rows, hub], axis=0)
        return jnp.broadcast_to(column, (bound + 2 * hubs, LO)).astype(BF16)

    list_high, list_low = digit(lambda v: v >> 8), digit(lambda v: v & (LO - 1))
    lane = lax.broadcasted_iota(jnp.int32, (bound + 2 * hubs, LO), 1).astype(F32).astype(BF16)
    for h in range(nodes // LO):
        low = jnp.where(list_high == jnp.full((), h, BF16), list_low, -one)
        picks[:, h * LO : (h + 1) * LO] = jnp.where(low == lane, one, zero)
    loads[2].wait()
    packed = dot(picks[...], features_ref[...], 1, 0)
    hub_tile = halves(packed[bound : bound + hubs])
    rows_send[...] = jnp.concatenate(
        [halves(packed[:bound]), jnp.broadcast_to(hub_tile, (peers, 16, LANES))], axis=1
    ).astype(BF16)
    rows_in[me] = rows_send[me]
    picks_copy = pltpu.make_async_copy(picks, picks_out, out_sem.at[1])
    picks_copy.start()
    pl.semaphore_wait(barrier, peers - 1)

    @pl.loop(1, peers)
    def _(p):
        peer = lax.rem(me + p, peers)
        pltpu.make_async_remote_copy(
            src_ref=rows_send.at[peer], dst_ref=rows_in.at[me],
            send_sem=row_sem.at[0], recv_sem=row_sem.at[1],
            device_id=(peer,), device_id_type=MESH,
        ).start()

    loads[3].wait()
    loads[4].wait()
    usable = lax.broadcasted_iota(jnp.int32, (fan, nodes), 0) < counts_ref[...]
    index = jnp.where(usable, index_ref[...], -1).astype(F32)
    for start in range(0, nodes, LANES):
        spread = jnp.concatenate([index[:, start : start + LANES]] * (LANES // fan), axis=0)
        spread_rows[start : start + LANES, :] = spread.T
    slot_of = lax.broadcasted_iota(jnp.int32, (groups, LANES), 1) // fan
    tiles = []
    for first in range(0, GROUP, LANES // fan):
        tile = spread_rows[pl.ds(first, groups, stride=GROUP), :]
        for j in range(1, LANES // fan):
            piece = spread_rows[pl.ds(first + j, groups, stride=GROUP), :]
            tile = jnp.where(slot_of == j, piece, tile)
        tiles.append(tile)
    grouped = jnp.concatenate(tiles, axis=1).astype(jnp.int32)
    high_rows[...] = (grouped >> 8).astype(F32)
    low_rows[...] = (grouped & (LO - 1)).astype(F32)
    pairs = GROUP * fan
    mine = (
        lax.broadcasted_iota(jnp.int32, (GROUP, pairs), 0)
        == lax.broadcasted_iota(jnp.int32, (GROUP, pairs), 1) // fan
    )
    low_ids = lax.broadcasted_iota(jnp.int32, (LO, pairs), 0).astype(F32).astype(BF16)

    @pl.loop(0, groups // UNROLL)
    def _(step):
        rows = pl.ds(pl.multiple_of(step * UNROLL, UNROLL), UNROLL)
        highs, lows = high_rows[rows, :], low_rows[rows, :]
        for group in range(UNROLL):
            high = jnp.broadcast_to(highs[group : group + 1, :], (GROUP, pairs)).astype(BF16)
            high = jnp.where(mine, high, -one)
            low = jnp.broadcast_to(lows[group : group + 1, :], (16, pairs)).astype(BF16)
            low = jnp.concatenate([low] * (LO // 16), axis=0)
            low_hot = jnp.where(low_ids == low, one, zero).astype(F8)
            high_hot = jnp.concatenate(
                [jnp.where(high == jnp.full((), h, BF16), one, zero) for h in range(blocks)],
                axis=0,
            ).astype(F8)
            counted = dot(high_hot, low_hot, 1, 1).astype(BF16)
            at = pl.ds(pl.multiple_of((step * UNROLL + group) * GROUP, GROUP), GROUP)
            for h in range(blocks):
                count[at, h * LO : (h + 1) * LO] = counted[16 * h : 16 * h + 16]

    summed[...] = dot(count[:, :nodes], features_ref[...], 1, 0)

    others = pl.ds(0, peers - 1)
    pltpu.make_async_copy(rows_in.at[others], rows_in.at[others], row_sem.at[1]).wait()
    arrived = rows_in[...].astype(F32)
    table = jnp.concatenate([joined(arrived[:, :16]), joined(arrived[:, 16:])], axis=0)
    total = summed[...] + dot(count[:, nodes:], table.astype(BF16), 1, 0)

    for load in loads[5:]:
        load.wait()
    inverse = 1.0 / counts_ref[...].astype(F32)
    column = jnp.concatenate(
        [
            jnp.broadcast_to(inverse[:, start : start + LANES], (LANES, LANES)).T
            for start in range(0, nodes, LANES)
        ],
        axis=0,
    )
    mean_all[...] = jnp.concatenate(
        [total[:, start : start + LANES] * column for start in range(0, width, LANES)], axis=1
    ).astype(BF16)
    pre = dot(features_ref[...], self_ref[...], 1, 0) + dot(mean_all[...], neighbour_ref[...], 1, 0)
    sig = jax.nn.sigmoid(pre)
    activations_ref[...] = (pre * sig).astype(BF16)
    grad_pre = (
        cotangent_ref[...].astype(F32) * sig * (1.0 + pre * (1.0 - sig))
    ).astype(BF16)
    grad_t[...] = grad_pre.T
    act_copy = pltpu.make_async_copy(activations_ref, activations_out, out_sem.at[0])
    act_copy.start()

    def to_pair(source, target, sem):
        return pltpu.make_async_remote_copy(
            src_ref=source.at[1 - core], dst_ref=target,
            send_sem=sem.at[0], recv_sem=sem.at[1],
            device_id=(me + 1 - 2 * core,), device_id_type=MESH,
        )

    def to_half(source, target, sem):
        @pl.loop(1, half)
        def _(p):
            to = lax.rem(my_half + p, half)
            pltpu.make_async_remote_copy(
                src_ref=source.at[to], dst_ref=target.at[my_half],
                send_sem=sem.at[0], recv_sem=sem.at[1],
                device_id=(to * 2 + core,), device_id_type=MESH,
            ).start()

    def wait_for(ref, amount, sem):
        part = ref.at[pl.ds(0, amount)]
        pltpu.make_async_copy(part, part, sem).wait()

    edge_t[...] = (dot(neighbour_ref[...], grad_t[...], 1, 0) * inverse).astype(BF16)

    part = halves(dot(edge_t[...], count[:, nodes:], 1, 0).T)
    for o in range(peers):
        hub_pair_send[o % 2, o // 2] = part[peers + o]
    hub_pair_copy = to_pair(hub_pair_send, hub_pair_in, hub_pair_sem)
    hub_pair_copy.start()
    part_send[...] = part[:peers].astype(BF16)
    part_in[me] = part_send[me]

    @pl.loop(1, peers)
    def _(p):
        peer = lax.rem(me + p, peers)
        pltpu.make_async_remote_copy(
            src_ref=part_send.at[peer], dst_ref=part_in.at[me],
            send_sem=part_sem.at[0], recv_sem=part_sem.at[1],
            device_id=(peer,), device_id_type=MESH,
        ).start()

    upper = dot(grad_t[...], features_ref[...], 1, 0).T
    lower = dot(grad_t[...], mean_all[...], 1, 0).T
    for o in range(peers):
        source = upper if o * share < width else lower
        start = o * share % width
        for i in range(width // LANES):
            pair_send[o % 2, o // 2, i * share : (i + 1) * share] = (
                source[start : start + share, i * LANES : (i + 1) * LANES]
            )
    pair_copy = to_pair(pair_send, pair_in, pair_sem)
    pair_copy.start()

    def local(first, last):
        at = slice(first * LO, last * LO)
        part = dot(edge_t[...], count[:, at], 1, 0) + dot(self_ref[...], grad_t[:, at], 1, 0)
        base[at, :] = part.T
        pltpu.make_async_copy(base.at[at], base_out.at[at], out_sem.at[2]).start()

    local_blocks = nodes // LO
    hub_pair_copy.wait_recv()
    hub_send[...] = (hub_pair_send[core] + hub_pair_in[...]).astype(BF16)

    to_half(hub_send, hub_in, hub_sem)
    local(0, local_blocks // 4)
    pair_copy.wait_recv()
    half_send[...] = (pair_send[core] + pair_in[...]).astype(BF16)
    to_half(half_send, half_in, half_sem)

    local(local_blocks // 4, local_blocks)

    half_in[my_half] = jnp.zeros(half_in.shape[1:], BF16)
    hub_in[my_half] = jnp.zeros(hub_in.shape[1:], BF16)
    wait_for(half_in, half - 1, half_sem.at[1])
    weights = pair_send[core, my_half] + pair_in[my_half]
    weights = weights + jnp.sum(half_in[...].astype(F32), axis=0)
    for i in range(width // LANES):
        weight_sum[:, i * LANES : (i + 1) * LANES] = weights[i * share : (i + 1) * share]
    wait_for(part_in, peers - 1, part_sem.at[1])
    wait_for(hub_in, half - 1, hub_sem.at[1])
    own_hub = hub_pair_send[core, my_half] + hub_pair_in[my_half]
    hub_sum = joined((own_hub + jnp.sum(hub_in[...].astype(F32), axis=0))[None])
    hub_high = hub_sum.astype(BF16).astype(F32)
    returned_t[...] = jnp.concatenate(
        [joined(part_in[...].astype(F32)), hub_high, hub_sum - hub_high], axis=0
    ).astype(BF16).T
    last = (
        pltpu.make_async_copy(returned_t, returned_out, out_sem.at[3]),
        pltpu.make_async_copy(weight_sum, weight_out, out_sem.at[4]),
    )
    for copy in last:
        copy.start()

    wait_for(rows_send, peers - 1, row_sem.at[0])
    wait_for(part_send, peers - 1, part_sem.at[0])
    pair_copy.wait_send()
    hub_pair_copy.wait_send()
    wait_for(half_send, half - 1, half_sem.at[0])
    wait_for(hub_send, half - 1, hub_sem.at[0])
    act_copy.wait()
    picks_copy.wait()
    pltpu.make_async_copy(base, base_out, out_sem.at[2]).wait()
    for copy in last:
        copy.wait()


def finish_kernel(
    activations_in, base_in, picks_in, returned_in, weights_in,
    activations_out, grads_out, weights_out,
    picks, returned_t, base, activations, weights, in_sem, out_sem,
):
    nodes = base.shape[0]
    step = nodes // FINISH_STEPS
    slices = [slice(start, start + step) for start in range(0, nodes, step)]
    returned_read = pltpu.make_async_copy(returned_in, returned_t, in_sem.at[0])
    reads = [
        (
            pltpu.make_async_copy(picks_in.at[:, at], picks.at[:, at], in_sem.at[3 + 2 * i]),
            pltpu.make_async_copy(base_in.at[at], base.at[at], in_sem.at[4 + 2 * i]),
        )
        for i, at in enumerate(slices)
    ]
    through = (
        pltpu.make_async_copy(activations_in, activations, in_sem.at[1]),
        pltpu.make_async_copy(weights_in, weights, in_sem.at[2]),
    )
    writes = (
        pltpu.make_async_copy(activations, activations_out, out_sem.at[0]),
        pltpu.make_async_copy(weights, weights_out, out_sem.at[1]),
    )
    for read in (returned_read,) + reads[0] + through + sum(reads[1:], ()):
        read.start()
    returned_read.wait()
    for i, at in enumerate(slices):
        for read in reads[i]:
            read.wait()
        base[at, :] = base[at, :] + dot(returned_t[...], picks[:, at], 1, 0).T
        pltpu.make_async_copy(base.at[at], grads_out.at[at], out_sem.at[2]).start()
        if i == 0:
            for read, write in zip(through, writes):
                read.wait()
                write.start()
    for write in writes:
        write.wait()
    pltpu.make_async_copy(base, grads_out, out_sem.at[2]).wait()


def body(
    features, self_weight, neighbour_weight, send_lists, hub_nodes, neighbours, counts, cotangent
):
    nodes, width = features.shape
    fan = neighbours.shape[1]
    peers = lax.axis_size("dom")
    per_peer = send_lists.shape[2]
    hubs = hub_nodes.shape[1]
    bound = peers * per_peer
    columns = nodes + bound + peers * hubs
    share = 2 * width // peers
    half = peers // 2
    dma = pltpu.SemaphoreType.DMA
    any_space = pl.BlockSpec(memory_space=pl.ANY)
    picked = bound + 2 * hubs
    activations, base, picks, returned, weights = pl.pallas_call(
        functools.partial(whole_kernel, peers),
        in_specs=[any_space] * 8,
        out_specs=[any_space] * 5,
        out_shape=[
            jax.ShapeDtypeStruct((nodes, width), BF16),
            jax.ShapeDtypeStruct((nodes, width), F32),
            jax.ShapeDtypeStruct((picked, nodes), BF16),
            jax.ShapeDtypeStruct((width, picked), BF16),
            jax.ShapeDtypeStruct((share, width), F32),
        ],
        scratch_shapes=[
            pltpu.VMEM((fan, nodes), jnp.int32),
            pltpu.VMEM((1, nodes), jnp.int32),
            pltpu.VMEM((per_peer, peers), jnp.int32),
            pltpu.VMEM((1, hubs), jnp.int32),
            pltpu.VMEM((nodes, width), BF16),
            pltpu.VMEM((nodes, width), BF16),
            pltpu.VMEM((width, width), BF16),
            pltpu.VMEM((width, width), BF16),
            pltpu.VMEM((picked, nodes), BF16),
            pltpu.VMEM((peers, 32, LANES), BF16),
            pltpu.VMEM((peers, 32, LANES), BF16),
            pltpu.VMEM((nodes, LANES), F32),
            pltpu.VMEM((nodes // GROUP, GROUP * fan), F32),
            pltpu.VMEM((nodes // GROUP, GROUP * fan), F32),
            pltpu.VMEM((nodes, columns), BF16),
            pltpu.VMEM((nodes, width), F32),
            pltpu.VMEM((nodes, width), BF16),
            pltpu.VMEM((width, nodes), BF16),
            pltpu.VMEM((width, nodes), BF16),
            pltpu.VMEM((nodes, width), BF16),
            pltpu.VMEM((nodes, width), F32),
            pltpu.VMEM((width, picked), BF16),
            pltpu.VMEM((share, width), F32),
            pltpu.VMEM((peers, 16, LANES), BF16),
            pltpu.VMEM((peers, 16, LANES), BF16),
            pltpu.VMEM((2, half, 2 * share, LANES), F32),
            pltpu.VMEM((half, 2 * share, LANES), F32),
            pltpu.VMEM((half, 2 * share, LANES), BF16),
            pltpu.VMEM((half, 2 * share, LANES), BF16),
            pltpu.VMEM((2, half, 16, LANES), F32),
            pltpu.VMEM((half, 16, LANES), F32),
            pltpu.VMEM((half, 16, LANES), BF16),
            pltpu.VMEM((half, 16, LANES), BF16),
            dma((8,)), dma((2,)), dma((2,)), dma((2,)), dma((2,)), dma((2,)), dma((2,)), dma((5,)),
        ],
        compiler_params=pltpu.CompilerParams(
            collective_id=0, has_side_effects=True, vmem_limit_bytes=VMEM_MAIN * 1024 * 1024
        ),
        name="whole",
    )(
        neighbours.T, counts[None, :], send_lists[0].T, hub_nodes, features, cotangent, self_weight,
        neighbour_weight,
    )
    return pl.pallas_call(
        finish_kernel,
        in_specs=[any_space] * 5,
        out_specs=[any_space] * 3,
        out_shape=[
            jax.ShapeDtypeStruct((nodes, width), BF16),
            jax.ShapeDtypeStruct((nodes, width), F32),
            jax.ShapeDtypeStruct((share, width), F32),
        ],
        scratch_shapes=[
            pltpu.VMEM((picked, nodes), BF16),
            pltpu.VMEM((width, picked), BF16),
            pltpu.VMEM((nodes, width), F32),
            pltpu.VMEM((nodes, width), BF16),
            pltpu.VMEM((share, width), F32),
            dma((3 + 2 * FINISH_STEPS,)), dma((3,)),
        ],
        compiler_params=pltpu.CompilerParams(vmem_limit_bytes=60 * 1024 * 1024),
        name="finish",
    )(activations, base, picks, returned, weights)


def solution(mesh):
    in_specs = (
        P("dom", None),
        P(),
        P(),
        P("dom", None, None),
        P("dom", None),
        P("dom", None),
        P("dom"),
        P("dom", None),
    )
    out_specs = (P("dom", None), P("dom", None), P("dom", None))
    return jax.shard_map(body, mesh=mesh, in_specs=in_specs, out_specs=out_specs, check_vma=False)
```

```python
import functools

import jax
import jax.numpy as jnp
from jax import lax
from jax.experimental import pallas as pl
from jax.experimental.pallas import tpu as pltpu
from jax.sharding import PartitionSpec as P

LO = 256
LANES = 128
VMEM_MAIN = 60
FINISH_STEPS = 2
GROUP = 16
UNROLL = 32
BF16 = jnp.bfloat16
F32 = jnp.float32
F8 = jnp.float8_e4m3fn
MESH = pl.DeviceIdType.MESH


def dot(a, b, ca, cb):
    return lax.dot_general(a, b, (((ca,), (cb,)), ((), ())), preferred_element_type=F32)


def halves(rows):
    count, width = rows.shape[0] // 8, rows.shape[1] // LANES
    return jnp.concatenate(
        [rows[:, i * LANES : (i + 1) * LANES].reshape(count, 8, LANES) for i in range(width)], axis=1
    )


def joined(tiles):
    count, width = tiles.shape[0], tiles.shape[1] // 8
    return jnp.concatenate(
        [tiles[:, i * 8 : (i + 1) * 8].reshape(count * 8, LANES) for i in range(width)], axis=1
    )


def whole_kernel(
    peers,
    neighbours_in, counts_in, lists_in, hubs_in, features_in, cotangent_in, self_in, neighbour_in,
    activations_out, base_out, picks_out, returned_out, weight_out,
    index_ref, counts_ref, lists_ref, hubs_ref, features_ref, cotangent_ref, self_ref, neighbour_ref,
    picks, rows_send, rows_in, spread_rows, high_rows, low_rows, count, summed, mean_all, grad_t, edge_t,
    activations_ref, base, returned_t, weight_sum, part_send, part_in,
    pair_send, pair_in, half_send, half_in, hub_pair_send, hub_pair_in, hub_send, hub_in,
    in_sem, row_sem, part_sem, pair_sem, half_sem, hub_pair_sem, hub_sem, out_sem,
):
    me = lax.axis_index("dom")
    core = me % 2
    half, my_half = peers // 2, me // 2
    nodes, width = features_ref.shape
    fan = index_ref.shape[0]
    per_peer = lists_ref.shape[0]
    hubs = hubs_ref.shape[1]
    bound = peers * per_peer
    groups = nodes // GROUP
    blocks = count.shape[1] // LO
    share = weight_sum.shape[0]

    ins = (
        (lists_in, lists_ref), (hubs_in, hubs_ref), (neighbours_in, index_ref),
        (counts_in, counts_ref), (features_in, features_ref), (self_in, self_ref),
        (neighbour_in, neighbour_ref), (cotangent_in, cotangent_ref),
    )
    loads = [pltpu.make_async_copy(a, b, in_sem.at[i]) for i, (a, b) in enumerate(ins)]
    for load in loads:
        load.start()

    barrier = pltpu.get_barrier_semaphore()

    @pl.loop(1, peers)
    def _(p):
        pl.semaphore_signal(
            barrier, inc=1, device_id=(lax.rem(me + p, peers),), device_id_type=MESH
        )

    one = jnp.ones((), BF16)
    zero = jnp.zeros((), BF16)

    loads[0].wait()
    loads[1].wait()
    owner = jnp.where(
        lax.broadcasted_iota(jnp.int32, (bound, peers), 0) // per_peer
        == lax.broadcasted_iota(jnp.int32, (bound, peers), 1), 1.0, 0.0,
    ).astype(BF16)
    own_slot = (
        lax.broadcasted_iota(jnp.int32, (bound, per_peer), 0) % per_peer
        == lax.broadcasted_iota(jnp.int32, (bound, per_peer), 1)
    )
    own_hub = (
        lax.broadcasted_iota(jnp.int32, (2 * hubs, hubs), 0) % hubs
        == lax.broadcasted_iota(jnp.int32, (2 * hubs, hubs), 1)
    )
    spread_hubs = jnp.broadcast_to(hubs_ref[...], (2 * hubs, hubs))

    def digit(take):
        sent = take(lists_ref[...]).astype(F32).astype(BF16)
        rows = jnp.sum(jnp.where(own_slot, dot(owner, sent, 1, 1), 0.0), axis=1, keepdims=True)
        hub = jnp.sum(
            jnp.where(own_hub, take(spread_hubs).astype(F32), 0.0), axis=1, keepdims=True
        )
        column = jnp.concatenate([rows, hub], axis=0)
        return jnp.broadcast_to(column, (bound + 2 * hubs, LO)).astype(BF16)

    list_high, list_low = digit(lambda v: v >> 8), digit(lambda v: v & (LO - 1))
    lane = lax.broadcasted_iota(jnp.int32, (bound + 2 * hubs, LO), 1).astype(F32).astype(BF16)
    for h in range(nodes // LO):
        low = jnp.where(list_high == jnp.full((), h, BF16), list_low, -one)
        picks[:, h * LO : (h + 1) * LO] = jnp.where(low == lane, one, zero)
    loads[2].wait()
    loads[3].wait()
    usable = lax.broadcasted_iota(jnp.int32, (fan, nodes), 0) < counts_ref[...]
    index = jnp.where(usable, index_ref[...], -1).astype(F32)
    for start in range(0, nodes, LANES):
        spread = jnp.concatenate([index[:, start : start + LANES]] * (LANES // fan), axis=0)
        spread_rows[start : start + LANES, :] = spread.T
    slot_of = lax.broadcasted_iota(jnp.int32, (groups, LANES), 1) // fan
    tiles = []
    for first in range(0, GROUP, LANES // fan):
        tile = spread_rows[pl.ds(first, groups, stride=GROUP), :]
        for j in range(1, LANES // fan):
            piece = spread_rows[pl.ds(first + j, groups, stride=GROUP), :]
            tile = jnp.where(slot_of == j, piece, tile)
        tiles.append(tile)
    grouped = jnp.concatenate(tiles, axis=1).astype(jnp.int32)
    high_rows[...] = (grouped >> 8).astype(F32)
    low_rows[...] = (grouped & (LO - 1)).astype(F32)
    loads[4].wait()
    packed = dot(picks[...], features_ref[...], 1, 0)
    hub_tile = halves(packed[bound : bound + hubs])
    rows_send[...] = jnp.concatenate(
        [halves(packed[:bound]), jnp.broadcast_to(hub_tile, (peers, 16, LANES))], axis=1
    ).astype(BF16)
    rows_in[me] = rows_send[me]
    picks_copy = pltpu.make_async_copy(picks, picks_out, out_sem.at[1])
    picks_copy.start()
    pl.semaphore_wait(barrier, peers - 1)

    @pl.loop(1, peers)
    def _(p):
        peer = lax.rem(me + p, peers)
        pltpu.make_async_remote_copy(
            src_ref=rows_send.at[peer], dst_ref=rows_in.at[me],
            send_sem=row_sem.at[0], recv_sem=row_sem.at[1],
            device_id=(peer,), device_id_type=MESH,
        ).start()

    pairs = GROUP * fan
    mine = (
        lax.broadcasted_iota(jnp.int32, (GROUP, pairs), 0)
        == lax.broadcasted_iota(jnp.int32, (GROUP, pairs), 1) // fan
    )
    low_ids = lax.broadcasted_iota(jnp.int32, (LO, pairs), 0).astype(F32).astype(BF16)

    @pl.loop(0, groups // UNROLL)
    def _(step):
        rows = pl.ds(pl.multiple_of(step * UNROLL, UNROLL), UNROLL)
        highs, lows = high_rows[rows, :], low_rows[rows, :]
        for group in range(UNROLL):
            high = jnp.broadcast_to(highs[group : group + 1, :], (GROUP, pairs)).astype(BF16)
            high = jnp.where(mine, high, -one)
            low = jnp.broadcast_to(lows[group : group + 1, :], (16, pairs)).astype(BF16)
            low = jnp.concatenate([low] * (LO // 16), axis=0)
            low_hot = jnp.where(low_ids == low, one, zero).astype(F8)
            high_hot = jnp.concatenate(
                [jnp.where(high == jnp.full((), h, BF16), one, zero) for h in range(blocks)],
                axis=0,
            ).astype(F8)
            counted = dot(high_hot, low_hot, 1, 1).astype(BF16)
            at = pl.ds(pl.multiple_of((step * UNROLL + group) * GROUP, GROUP), GROUP)
            for h in range(blocks):
                count[at, h * LO : (h + 1) * LO] = counted[16 * h : 16 * h + 16]

    summed[...] = dot(count[:, :nodes], features_ref[...], 1, 0)

    others = pl.ds(0, peers - 1)
    pltpu.make_async_copy(rows_in.at[others], rows_in.at[others], row_sem.at[1]).wait()
    arrived = rows_in[...].astype(F32)
    table = jnp.concatenate([joined(arrived[:, :16]), joined(arrived[:, 16:])], axis=0)
    total = summed[...] + dot(count[:, nodes:], table.astype(BF16), 1, 0)

    for load in loads[5:]:
        load.wait()
    inverse = 1.0 / counts_ref[...].astype(F32)
    column = jnp.concatenate(
        [
            jnp.broadcast_to(inverse[:, start : start + LANES], (LANES, LANES)).T
            for start in range(0, nodes, LANES)
        ],
        axis=0,
    )
    mean_all[...] = jnp.concatenate(
        [total[:, start : start + LANES] * column for start in range(0, width, LANES)], axis=1
    ).astype(BF16)
    pre = dot(features_ref[...], self_ref[...], 1, 0) + dot(mean_all[...], neighbour_ref[...], 1, 0)
    sig = jax.nn.sigmoid(pre)
    activations_ref[...] = (pre * sig).astype(BF16)
    grad_pre = (
        cotangent_ref[...].astype(F32) * sig * (1.0 + pre * (1.0 - sig))
    ).astype(BF16)
    grad_t[...] = grad_pre.T
    act_copy = pltpu.make_async_copy(activations_ref, activations_out, out_sem.at[0])
    act_copy.start()

    def to_pair(source, target, sem):
        return pltpu.make_async_remote_copy(
            src_ref=source.at[1 - core], dst_ref=target,
            send_sem=sem.at[0], recv_sem=sem.at[1],
            device_id=(me + 1 - 2 * core,), device_id_type=MESH,
        )

    def to_half(source, target, sem):
        @pl.loop(1, half)
        def _(p):
            to = lax.rem(my_half + p, half)
            pltpu.make_async_remote_copy(
                src_ref=source.at[to], dst_ref=target.at[my_half],
                send_sem=sem.at[0], recv_sem=sem.at[1],
                device_id=(to * 2 + core,), device_id_type=MESH,
            ).start()

    def wait_for(ref, amount, sem):
        part = ref.at[pl.ds(0, amount)]
        pltpu.make_async_copy(part, part, sem).wait()

    edge_t[...] = (dot(neighbour_ref[...], grad_t[...], 1, 0) * inverse).astype(BF16)

    part = halves(dot(edge_t[...], count[:, nodes:], 1, 0).T)
    for o in range(peers):
        hub_pair_send[o % 2, o // 2] = part[peers + o]
    hub_pair_copy = to_pair(hub_pair_send, hub_pair_in, hub_pair_sem)
    hub_pair_copy.start()
    part_send[...] = part[:peers].astype(BF16)
    part_in[me] = part_send[me]

    @pl.loop(1, peers)
    def _(p):
        peer = lax.rem(me + p, peers)
        pltpu.make_async_remote_copy(
            src_ref=part_send.at[peer], dst_ref=part_in.at[me],
            send_sem=part_sem.at[0], recv_sem=part_sem.at[1],
            device_id=(peer,), device_id_type=MESH,
        ).start()

    both = jnp.concatenate([features_ref[...], mean_all[...]], axis=1)
    both = dot(grad_t[...], both, 1, 0).T
    for o in range(peers):
        start = o * share
        for i in range(width // LANES):
            pair_send[o % 2, o // 2, i * share : (i + 1) * share] = (
                both[start : start + share, i * LANES : (i + 1) * LANES]
            )
    pair_copy = to_pair(pair_send, pair_in, pair_sem)
    pair_copy.start()

    def local(first, last):
        at = slice(first * LO, last * LO)
        part = dot(edge_t[...], count[:, at], 1, 0) + dot(self_ref[...], grad_t[:, at], 1, 0)
        base[at, :] = part.T
        pltpu.make_async_copy(base.at[at], base_out.at[at], out_sem.at[2]).start()

    local_blocks = nodes // LO
    hub_pair_copy.wait_recv()
    hub_send[...] = (hub_pair_send[core] + hub_pair_in[...]).astype(BF16)

    to_half(hub_send, hub_in, hub_sem)
    local(0, local_blocks // 4)
    pair_copy.wait_recv()
    half_send[...] = (pair_send[core] + pair_in[...]).astype(BF16)
    to_half(half_send, half_in, half_sem)

    local(local_blocks // 4, local_blocks)

    half_in[my_half] = jnp.zeros(half_in.shape[1:], BF16)
    hub_in[my_half] = jnp.zeros(hub_in.shape[1:], BF16)
    wait_for(half_in, half - 1, half_sem.at[1])
    weights = pair_send[core, my_half] + pair_in[my_half]
    weights = weights + jnp.sum(half_in[...].astype(F32), axis=0)
    for i in range(width // LANES):
        weight_sum[:, i * LANES : (i + 1) * LANES] = weights[i * share : (i + 1) * share]
    wait_for(part_in, peers - 1, part_sem.at[1])
    wait_for(hub_in, half - 1, hub_sem.at[1])
    own_hub = hub_pair_send[core, my_half] + hub_pair_in[my_half]
    hub_sum = joined((own_hub + jnp.sum(hub_in[...].astype(F32), axis=0))[None])
    hub_high = hub_sum.astype(BF16).astype(F32)
    returned_t[...] = jnp.concatenate(
        [joined(part_in[...].astype(F32)), hub_high, hub_sum - hub_high], axis=0
    ).astype(BF16).T
    last = (
        pltpu.make_async_copy(returned_t, returned_out, out_sem.at[3]),
        pltpu.make_async_copy(weight_sum, weight_out, out_sem.at[4]),
    )
    for copy in last:
        copy.start()

    wait_for(rows_send, peers - 1, row_sem.at[0])
    wait_for(part_send, peers - 1, part_sem.at[0])
    pair_copy.wait_send()
    hub_pair_copy.wait_send()
    wait_for(half_send, half - 1, half_sem.at[0])
    wait_for(hub_send, half - 1, hub_sem.at[0])
    act_copy.wait()
    picks_copy.wait()
    pltpu.make_async_copy(base, base_out, out_sem.at[2]).wait()
    for copy in last:
        copy.wait()


def finish_kernel(
    activations_in, base_in, picks_in, returned_in, weights_in,
    activations_out, grads_out, weights_out,
    picks, returned_t, base, activations, weights, in_sem, out_sem,
):
    nodes = base.shape[0]
    step = nodes // FINISH_STEPS
    slices = [slice(start, start + step) for start in range(0, nodes, step)]
    returned_read = pltpu.make_async_copy(returned_in, returned_t, in_sem.at[0])
    reads = [
        (
            pltpu.make_async_copy(picks_in.at[:, at], picks.at[:, at], in_sem.at[3 + 2 * i]),
            pltpu.make_async_copy(base_in.at[at], base.at[at], in_sem.at[4 + 2 * i]),
        )
        for i, at in enumerate(slices)
    ]
    through = (
        pltpu.make_async_copy(activations_in, activations, in_sem.at[1]),
        pltpu.make_async_copy(weights_in, weights, in_sem.at[2]),
    )
    writes = (
        pltpu.make_async_copy(activations, activations_out, out_sem.at[0]),
        pltpu.make_async_copy(weights, weights_out, out_sem.at[1]),
    )
    for read in (returned_read,) + reads[0] + through + sum(reads[1:], ()):
        read.start()
    returned_read.wait()
    for i, at in enumerate(slices):
        for read in reads[i]:
            read.wait()
        base[at, :] = base[at, :] + dot(returned_t[...], picks[:, at], 1, 0).T
        pltpu.make_async_copy(base.at[at], grads_out.at[at], out_sem.at[2]).start()
        if i == 0:
            for read, write in zip(through, writes):
                read.wait()
                write.start()
    for write in writes:
        write.wait()
    pltpu.make_async_copy(base, grads_out, out_sem.at[2]).wait()


def body(
    features, self_weight, neighbour_weight, send_lists, hub_nodes, neighbours, counts, cotangent
):
    nodes, width = features.shape
    fan = neighbours.shape[1]
    peers = lax.axis_size("dom")
    per_peer = send_lists.shape[2]
    hubs = hub_nodes.shape[1]
    bound = peers * per_peer
    columns = nodes + bound + peers * hubs
    share = 2 * width // peers
    half = peers // 2
    dma = pltpu.SemaphoreType.DMA
    any_space = pl.BlockSpec(memory_space=pl.ANY)
    picked = bound + 2 * hubs
    activations, base, picks, returned, weights = pl.pallas_call(
        functools.partial(whole_kernel, peers),
        in_specs=[any_space] * 8,
        out_specs=[any_space] * 5,
        out_shape=[
            jax.ShapeDtypeStruct((nodes, width), BF16),
            jax.ShapeDtypeStruct((nodes, width), F32),
            jax.ShapeDtypeStruct((picked, nodes), BF16),
            jax.ShapeDtypeStruct((width, picked), BF16),
            jax.ShapeDtypeStruct((share, width), F32),
        ],
        scratch_shapes=[
            pltpu.VMEM((fan, nodes), jnp.int32),
            pltpu.VMEM((1, nodes), jnp.int32),
            pltpu.VMEM((per_peer, peers), jnp.int32),
            pltpu.VMEM((1, hubs), jnp.int32),
            pltpu.VMEM((nodes, width), BF16),
            pltpu.VMEM((nodes, width), BF16),
            pltpu.VMEM((width, width), BF16),
            pltpu.VMEM((width, width), BF16),
            pltpu.VMEM((picked, nodes), BF16),
            pltpu.VMEM((peers, 32, LANES), BF16),
            pltpu.VMEM((peers, 32, LANES), BF16),
            pltpu.VMEM((nodes, LANES), F32),
            pltpu.VMEM((nodes // GROUP, GROUP * fan), F32),
            pltpu.VMEM((nodes // GROUP, GROUP * fan), F32),
            pltpu.VMEM((nodes, columns), BF16),
            pltpu.VMEM((nodes, width), F32),
            pltpu.VMEM((nodes, width), BF16),
            pltpu.VMEM((width, nodes), BF16),
            pltpu.VMEM((width, nodes), BF16),
            pltpu.VMEM((nodes, width), BF16),
            pltpu.VMEM((nodes, width), F32),
            pltpu.VMEM((width, picked), BF16),
            pltpu.VMEM((share, width), F32),
            pltpu.VMEM((peers, 16, LANES), BF16),
            pltpu.VMEM((peers, 16, LANES), BF16),
            pltpu.VMEM((2, half, 2 * share, LANES), F32),
            pltpu.VMEM((half, 2 * share, LANES), F32),
            pltpu.VMEM((half, 2 * share, LANES), BF16),
            pltpu.VMEM((half, 2 * share, LANES), BF16),
            pltpu.VMEM((2, half, 16, LANES), F32),
            pltpu.VMEM((half, 16, LANES), F32),
            pltpu.VMEM((half, 16, LANES), BF16),
            pltpu.VMEM((half, 16, LANES), BF16),
            dma((8,)), dma((2,)), dma((2,)), dma((2,)), dma((2,)), dma((2,)), dma((2,)), dma((5,)),
        ],
        compiler_params=pltpu.CompilerParams(
            collective_id=0, has_side_effects=True, vmem_limit_bytes=VMEM_MAIN * 1024 * 1024
        ),
        name="whole",
    )(
        neighbours.T, counts[None, :], send_lists[0].T, hub_nodes, features, cotangent, self_weight,
        neighbour_weight,
    )
    return pl.pallas_call(
        finish_kernel,
        in_specs=[any_space] * 5,
        out_specs=[any_space] * 3,
        out_shape=[
            jax.ShapeDtypeStruct((nodes, width), BF16),
            jax.ShapeDtypeStruct((nodes, width), F32),
            jax.ShapeDtypeStruct((share, width), F32),
        ],
        scratch_shapes=[
            pltpu.VMEM((picked, nodes), BF16),
            pltpu.VMEM((width, picked), BF16),
            pltpu.VMEM((nodes, width), F32),
            pltpu.VMEM((nodes, width), BF16),
            pltpu.VMEM((share, width), F32),
            dma((3 + 2 * FINISH_STEPS,)), dma((3,)),
        ],
        compiler_params=pltpu.CompilerParams(vmem_limit_bytes=60 * 1024 * 1024),
        name="finish",
    )(activations, base, picks, returned, weights)


def solution(mesh):
    in_specs = (
        P("dom", None),
        P(),
        P(),
        P("dom", None, None),
        P("dom", None),
        P("dom", None),
        P("dom"),
        P("dom", None),
    )
    out_specs = (P("dom", None), P("dom", None), P("dom", None))
    return jax.shard_map(body, mesh=mesh, in_specs=in_specs, out_specs=out_specs, check_vma=False)
```
